128 devices in a mesh: row: 8 (over y, x_lo), col: 16 (over x_hi, z, core).
Axes of the slice: x: 4 (x_hi: 2, x_lo: 2; x = x_hi * 2 + x_lo), y: 4, z: 4, core: 2. Of those that a mesh axis runs over, the one named last changes fastest.
Arguments:
- activations: bfloat16 [2048, 8192], P('col', 'row'), may hold values from -6 to 6
- output_grad: bfloat16 [2048, 8192], P('col', 'row'), may hold values from -1.5 to 1.5
- tile_counts: int32 [32], replicated, may hold values from 16 to 64, as said below
- w_gate: bfloat16 [8192, 15360], P('row', 'col'), may hold values from -0.0625 to 0.0625
- w_up: bfloat16 [8192, 15360], P('row', 'col'), may hold values from -0.0625 to 0.0625
- w_down: bfloat16 [15360, 8192], P('col', 'row'), may hold values from -0.046875 to 0.046875
Outputs:
- input_grad: bfloat16 [2048, 8192], P('col', 'row')
- grad_gate: bfloat16 [8192, 15360], P('row', 'col')
- grad_up: bfloat16 [8192, 15360], P('row', 'col')
- grad_down: bfloat16 [15360, 8192], P('col', 'row')
The draws below stay inside these ranges and needn't reach their ends.
Inputs may be any that keep to these rules, and one draw needn't show every extreme that they name: `tile_counts`: number of live tokens at the start of each tile of 64 positions; some tile is full and some holds 16.
All inputs are finite; a program needn't handle non-finite values.
Results may differ from the reference program's by a relative error of at most 0.03.
Values may be sent and summed in bfloat16 or wider, within the bound.
No kernel may reach another device: no remote copies, remote signals or barrier semaphores. Data moves between devices by JAX's collectives and lax.ppermute only.
A program may use at most 128 MiB of HBM per device.

```python
import jax
import jax.numpy as jnp
from jax import lax

D = 8192
FF = 15360
TILE = 64
TOKENS = 2048
TILES = 32
D_BLK = 1024
N_ROW = 8


def draw_tile_counts(key, part):
    first_key, second_key = jax.random.split(key, 2)
    counts = jax.random.randint(first_key, (TILES,), TILE // 4, TILE + 1)
    order = jax.random.permutation(second_key, TILES)
    counts = counts.at[order[0]].set(TILE)
    counts = counts.at[order[1]].set(TILE // 4)
    return counts.astype(jnp.int32)


def block_levels(stream_key, extent, cuts, low, largest):
    gain, own = 1.0, jax.random.fold_in(stream_key, 6)
    for dim, parts in cuts:
        steps = jnp.exp(jax.random.uniform(jax.random.fold_in(own, dim), (parts,), jnp.float32, low / len(cuts), largest / len(cuts)))
        gain = gain * jnp.repeat(steps, extent[dim] // parts).reshape([-1 if axis == dim else 1 for axis in range(len(extent))])
    return gain


def gaussian(key, extent, spread, bound, shards=(), kind=jnp.bfloat16):
    entries = spread * jax.random.normal(key, extent, jnp.float32)
    if shards:
        entries = entries * block_levels(key, extent, shards, -0.22, 0.18)
    return jnp.clip(entries, -bound, bound).astype(kind)


def setup_inputs(seed: int = 0) -> dict:
    key_of = jax.random.split(jax.random.key(seed), 7)
    activations = gaussian(key_of[0], (TOKENS, D), 1.0, 6.0, ((0, 16), (1, 8)))
    output_grad = gaussian(key_of[1], (TOKENS, D), 0.25, 1.5, ((0, 16), (1, 8)))
    tile_counts = draw_tile_counts(jax.random.fold_in(key_of[6], 71), 0)
    w_gate = gaussian(key_of[3], (D, FF), D ** -0.5, 0.0625, ((0, 8), (1, 16)))
    w_up = gaussian(key_of[4], (D, FF), D ** -0.5, 0.0625, ((0, 8), (1, 16)))
    w_down = gaussian(key_of[5], (FF, D), FF ** -0.5, 0.046875, ((0, 16), (1, 8)))
    return dict(activations=activations, output_grad=output_grad, tile_counts=tile_counts, w_gate=w_gate, w_up=w_up, w_down=w_down)


def settle(values):
    return lax.optimization_barrier(values.astype(jnp.bfloat16)).astype(jnp.float32)


def reference(activations, output_grad, tile_counts, w_gate, w_up, w_down):
    position = jnp.arange(TOKENS, dtype=jnp.int32)
    row_limit = tile_counts[position // TILE]
    kept_rows = (position % TILE) < row_limit
    live_grad = jnp.where(kept_rows[:, None], output_grad, jnp.zeros_like(output_grad))
    gate_sum = jnp.zeros((TOKENS, FF), jnp.float32)
    up_sum = jnp.zeros((TOKENS, FF), jnp.float32)
    back_sum = jnp.zeros((TOKENS, FF), jnp.float32)
    for block_idx in range(N_ROW):
        low_edge = block_idx * D_BLK
        input_block = activations[:, low_edge:low_edge + D_BLK]
        grad_block = live_grad[:, low_edge:low_edge + D_BLK]
        gate_sum = gate_sum + settle(jnp.dot(input_block, w_gate[low_edge:low_edge + D_BLK, :], preferred_element_type=jnp.float32))
        up_sum = up_sum + settle(jnp.dot(input_block, w_up[low_edge:low_edge + D_BLK, :], preferred_element_type=jnp.float32))
        back_sum = back_sum + settle(jnp.dot(grad_block, w_down[:, low_edge:low_edge + D_BLK].T, preferred_element_type=jnp.float32))
    sigmoid_gate = jax.nn.sigmoid(gate_sum)
    hidden = (gate_sum * sigmoid_gate * up_sum).astype(jnp.bfloat16)
    d_gate = (back_sum * up_sum * sigmoid_gate * (1.0 + gate_sum * (1.0 - sigmoid_gate))).astype(jnp.bfloat16)
    d_up = (back_sum * gate_sum * sigmoid_gate).astype(jnp.bfloat16)
    input_grad = (jnp.dot(d_gate, w_gate.T, preferred_element_type=jnp.float32) + jnp.dot(d_up, w_up.T, preferred_element_type=jnp.float32)).astype(jnp.bfloat16)
    grad_gate = jnp.dot(activations.T, d_gate, preferred_element_type=jnp.float32).astype(jnp.bfloat16)
    grad_up = jnp.dot(activations.T, d_up, preferred_element_type=jnp.float32).astype(jnp.bfloat16)
    grad_down = jnp.dot(hidden.T, live_grad, preferred_element_type=jnp.float32).astype(jnp.bfloat16)
    return (input_grad, grad_gate, grad_up, grad_down)
```

```python
import jax
import jax.numpy as jnp
from jax import lax
from jax.sharding import Mesh, PartitionSpec as P

TILE = 64
GROUPS = 4
BF = jnp.bfloat16
F32 = jnp.float32


def dot(left, right, dims):
    return lax.dot_general(left, right, ((dims[:1], dims[1:]), ((), ())), preferred_element_type=F32)


def shift(value, axis, size, step):
    return lax.ppermute(value, axis, [(i, (i + step) % size) for i in range(size)])


def gather_col(value, z_first):
    if z_first:
        blocks = [value] + [shift(value, "z", 4, -k) for k in (1, 2, 3)]
        near = jnp.concatenate(blocks, axis=0)
        far = shift(near, "xh", 2, 1)
    else:
        pair = jnp.concatenate([value, shift(value, "xh", 2, 1)], axis=0)
        moved = [pair] + [shift(pair, "z", 4, -k) for k in (1, 2, 3)]
        rows = value.shape[0]
        near = jnp.concatenate([m[:rows] for m in moved], axis=0)
        far = jnp.concatenate([m[rows:] for m in moved], axis=0)
    half = jnp.concatenate([near, far], axis=0)
    return jnp.concatenate([half, shift(half, "c", 2, 1)], axis=0)


def scatter_col(part):
    rows = part.shape[0] // 16
    half = part.shape[0] // 2
    own = part[:half].astype(BF).astype(F32) + shift(part[half:].astype(BF), "c", 2, 1).astype(F32)
    quarter = half // 2
    own = own[:quarter] + shift(own[quarter:].astype(BF), "xh", 2, 1).astype(F32)
    out = own[:rows]
    for k in (1, 2, 3):
        out = out + shift(own[k * rows : (k + 1) * rows].astype(BF), "z", 4, k).astype(F32)
    return out.astype(BF)


def scatter_row_y(parts, low, rows):
    def block(k, width, skip=0):
        start = low + k * 2 * rows + skip
        return jnp.stack([p[start : start + width] for p in parts])

    total = block(0, 2 * rows).astype(F32)
    for k in (1, 2, 3):
        total = total + shift(block(k, 2 * rows), "y", 4, k).astype(F32)
    return total[:, :rows] + shift(total[:, rows:].astype(BF), "xl", 2, 1).astype(F32)


def scatter_row_x(parts, low, rows):
    far = jnp.stack([p[low + 4 * rows : low + 8 * rows] for p in parts])
    near = jnp.stack([p[low : low + 4 * rows] for p in parts])
    total = near.astype(F32) + shift(far, "xl", 2, 1).astype(F32)
    out = total[:, :rows]
    for k in (1, 2, 3):
        out = out + shift(total[:, k * rows : (k + 1) * rows].astype(BF), "y", 4, k).astype(F32)
    return out


def gather_row_y(share):
    pair = jnp.concatenate([share, shift(share, "xl", 2, 1)], axis=1)
    return [pair] + [shift(pair, "y", 4, -k) for k in (1, 2, 3)]


def gather_row_x(share):
    near = jnp.concatenate([share] + [shift(share, "y", 4, -k) for k in (1, 2, 3)], axis=1)
    return [near, shift(near, "xl", 2, 1)]


def swiglu_back(totals):
    gate_sum, up_sum, back_sum = totals[0], totals[1], totals[2]
    sigmoid_gate = jax.nn.sigmoid(gate_sum)
    hidden = gate_sum * sigmoid_gate * up_sum
    d_gate = back_sum * up_sum * sigmoid_gate * (1.0 + gate_sum * (1.0 - sigmoid_gate))
    d_up = back_sum * gate_sum * sigmoid_gate
    return jnp.stack([hidden.astype(BF), d_gate.astype(BF), d_up.astype(BF)])


def to_relative(value, y, xl, rows_y, rows_x):
    first = value[: 8 * rows_y].reshape(4, 2, rows_y, -1)
    second = value[8 * rows_y :].reshape(2, 4, rows_x, -1)
    first = jnp.where(xl == 0, first, first[:, ::-1])
    second = jnp.where(xl == 0, second, second[::-1])
    first = lax.dynamic_slice_in_dim(jnp.concatenate([first, first[:3]], 0), y, 4, 0)
    second = lax.dynamic_slice_in_dim(jnp.concatenate([second, second[:, :3]], 1), y, 4, 1)
    width = value.shape[1]
    return jnp.concatenate([first.reshape(-1, width), second.reshape(-1, width)], 0)


def from_relative(value, y, xl, rows_y, rows_x):
    first = value[: 8 * rows_y].reshape(4, 2, rows_y, -1)
    second = value[8 * rows_y :].reshape(2, 4, rows_x, -1)
    first = jnp.where(xl == 0, first, first[:, ::-1])
    second = jnp.where(xl == 0, second, second[::-1])
    back = (4 - y) % 4
    first = lax.dynamic_slice_in_dim(jnp.concatenate([first, first[:3]], 0), back, 4, 0)
    second = lax.dynamic_slice_in_dim(jnp.concatenate([second, second[:, :3]], 1), back, 4, 1)
    width = value.shape[1]
    return jnp.concatenate([first.reshape(-1, width), second.reshape(-1, width)], 0)


def shards(activations, output_grad, tile_counts, w_gate, w_up, w_down):
    own_rows, width = activations.shape
    tiles = own_rows // TILE
    slots = TILE // GROUPS
    y, xl = lax.axis_index("y"), lax.axis_index("xl")
    col = lax.axis_index(("xh", "z", "c"))
    position = lax.iota(jnp.int32, own_rows)
    in_tile = (col * tiles + position // TILE)[:, None] == lax.iota(jnp.int32, tile_counts.shape[0])[None, :]
    row_limit = jnp.sum(jnp.where(in_tile, tile_counts[None, :], 0), axis=1)
    kept_rows = position % TILE < row_limit
    live_grad = jnp.where(kept_rows[:, None], output_grad, jnp.zeros_like(output_grad))
    acts = activations.reshape(tiles, GROUPS, slots, width)
    grads = live_grad.reshape(tiles, GROUPS, slots, width)
    chunk = 16 * tiles * slots
    rows_y = 3 * chunk // 64
    rows_x = chunk // 8 - rows_y
    wg = wu = wd = None
    out_grads = []
    for j in range(GROUPS):
        x = gather_col(acts[:, j].reshape(tiles * slots, width), True)
        g = gather_col(grads[:, j].reshape(tiles * slots, width), False)
        x = to_relative(x, y, xl, rows_y, rows_x)
        g = to_relative(g, y, xl, rows_y, rows_x)
        parts = (
            dot(x, w_gate, (1, 0)).astype(BF),
            dot(x, w_up, (1, 0)).astype(BF),
            dot(g, w_down, (1, 1)).astype(BF),
        )
        share_y = swiglu_back(scatter_row_y(parts, 0, rows_y))
        share_x = swiglu_back(scatter_row_x(parts, 8 * rows_y, rows_x))
        blocks = gather_row_y(share_y) + gather_row_x(share_x)
        hidden, d_gate, d_up = (jnp.concatenate([b[i] for b in blocks], axis=0) for i in range(3))
        part = (dot(d_gate, w_gate, (1, 1)) + dot(d_up, w_up, (1, 1))).astype(BF)
        out_grads.append(scatter_col(from_relative(part, y, xl, rows_y, rows_x)))
        new_g, new_u, new_d = dot(x, d_gate, (0, 0)), dot(x, d_up, (0, 0)), dot(hidden, g, (0, 0))
        wg, wu, wd = (new_g, new_u, new_d) if wg is None else (wg + new_g, wu + new_u, wd + new_d)
    input_grad = jnp.stack([o.reshape(tiles, slots, width) for o in out_grads], axis=1).reshape(own_rows, width)
    return (input_grad, wg.astype(BF), wu.astype(BF), wd.astype(BF))


def solution(mesh):
    fine = Mesh(mesh.devices.reshape(4, 2, 2, 4, 2), ("y", "xl", "xh", "z", "c"))
    row, col = ("y", "xl"), ("xh", "z", "c")
    in_specs = (P(col, row), P(col, row), P(), P(row, col), P(row, col), P(col, row))
    out_specs = (P(col, row), P(row, col), P(row, col), P(col, row))
    return jax.shard_map(shards, mesh=fine, in_specs=in_specs, out_specs=out_specs, check_vma=False)
```

```python
import jax
import jax.numpy as jnp
from jax import lax
from jax.experimental import pallas as pl
from jax.experimental.pallas import tpu as pltpu
from jax.sharding import Mesh, PartitionSpec as P

TILE = 64
HEAD = 16
CAP = 1024
BF = jnp.bfloat16
F32 = jnp.float32


def dot(left, right, dims):
    return lax.dot_general(left, right, ((dims[:1], dims[1:]), ((), ())), preferred_element_type=F32)


def shift(value, axis, size, step):
    return lax.ppermute(value, axis, [(i, (i + step) % size) for i in range(size)])


def move(place, sources, shapes, copies):
    count = len(copies(0, 0))

    def kernel(place_ref, *refs):
        ins, outs, sems = refs[: len(sources)], refs[len(sources) : -1], refs[-1]
        jobs = [
            pltpu.make_async_copy(ins[i].at[src], outs[o].at[dst], sems.at[n])
            for n, (o, dst, i, src) in enumerate(copies(place_ref[0], place_ref[1]))
        ]
        for job in jobs:
            job.start()
        for job in jobs:
            job.wait()

    anywhere = pl.BlockSpec(memory_space=pl.ANY)
    return pl.pallas_call(
        kernel,
        out_shape=[jax.ShapeDtypeStruct(s, BF) for s in shapes],
        in_specs=[pl.BlockSpec(memory_space=pltpu.SMEM)] + [anywhere] * len(sources),
        out_specs=[pl.BlockSpec(memory_space=pltpu.VMEM)] * len(shapes),
        scratch_shapes=[pltpu.SemaphoreType.DMA((count,))],
    )(place, *sources)


def after(token, *values):
    return lax.optimization_barrier((*values, token))[:-1]


def blank(shapes):
    return pl.pallas_call(
        lambda *refs: None,
        out_shape=[jax.ShapeDtypeStruct(s, BF) for s in shapes],
        out_specs=[pl.BlockSpec(memory_space=pl.ANY)] * len(shapes),
    )()


def span(start, size):
    return pl.ds(start if isinstance(start, int) else pl.multiple_of(start, 8), size)


def join(place, blocks):
    rows, width = blocks[0].shape
    return move(place, blocks, [(len(blocks) * rows, width)], lambda y, xl: [(0, span(n * rows, rows), n, span(0, rows)) for n in range(len(blocks))])[0]


def by_core(place, moved, rows):
    return move(
        place, moved, [(8 * rows, moved[0].shape[1])],
        lambda y, xl: [(0, span((4 * d + n) * rows, rows), n, span(d * rows, rows)) for n in range(4) for d in (0, 1)],
    )[0]


def over_z(value):
    return [value] + [shift(value, "z", 4, -k) for k in (1, 2, 3)]


def project(place, sources, weights, rows, y_first):
    units, width = weights[0].shape
    wide = -(-units // 128) * 128
    compact = len(sources) > 2
    total = 8 * rows
    if y_first:
        cuts = [(k * 2 * rows, 2 * rows) for k in range(4)]
    else:
        cuts = [(n * 4 * rows, 4 * rows) for n in range(2)]
    shapes = [(3, size, wide) for _, size in cuts]
    if compact:
        shapes = [(total, width)] * 2 + shapes
    n_in = len(sources) + 3

    def kernel(place_ref, *refs):
        ins, w_refs, outs = refs[: len(sources)], refs[len(sources) : n_in], refs[n_in : n_in + len(shapes)]
        bufs, sems = refs[n_in + len(shapes) : -1], refs[-1]
        jobs = []

        def start(src, dst):
            job = pltpu.make_async_copy(src, dst, sems.at[len(jobs)])
            job.start()
            jobs.append(job)
            return job

        if compact:
            rank = ins[0][...]
            feeds = [start(ins[1 + i], bufs[3 + i]) for i in range(4)]
        else:
            feeds = []
            for i in (0, 1):
                for k in range(4):
                    for d in (0, 1):
                        block = ((place_ref[0] + k) % 4) * 2 + (place_ref[1] + d) % 2
                        feeds.append(start(ins[i].at[span(block * rows, rows)], bufs[3 + i].at[span((2 * k + d) * rows, rows)]))
        loads = [start(w_refs[i], bufs[i]) for i in range(3)]
        if compact:
            pick = (lax.broadcasted_iota(jnp.int32, (total, rank.shape[1]), 0) == rank).astype(F32).astype(BF)
            half = rank.shape[1] // 2
            for i in (0, 1):
                feeds[2 * i].wait()
                feeds[2 * i + 1].wait()
                outs[i][...] = (dot(pick[:, :half], bufs[3 + 2 * i][...], (1, 0)) + dot(pick[:, half:], bufs[4 + 2 * i][...], (1, 0))).astype(BF)
            lefts = outs[:2]
            packs = outs[2:]
        else:
            for feed in feeds:
                feed.wait()
            lefts = bufs[3:5]
            packs = outs
        for i in range(3):
            loads[i].wait()
            for (low, size), out in zip(cuts, packs):
                left = lefts[i // 2][low : low + size]
                out[i, :, :units] = dot(left, bufs[i][...], (1, 1)).astype(BF)
                out[i, :, units:] = jnp.zeros((size, wide - units), BF)

    anywhere = pl.BlockSpec(memory_space=pl.ANY)
    vmem = pl.BlockSpec(memory_space=pltpu.VMEM)
    smem = pl.BlockSpec(memory_space=pltpu.SMEM)
    scratch = [pltpu.VMEM(w.shape, BF) for w in weights]
    scratch += [pltpu.VMEM(s.shape, BF) for s in (sources[1:] if compact else sources)]
    return pl.pallas_call(
        kernel,
        out_shape=[jax.ShapeDtypeStruct(s, BF) for s in shapes],
        in_specs=[smem] + ([vmem] if compact else []) + [anywhere] * (n_in - compact),
        out_specs=[vmem] * len(shapes),
        scratch_shapes=scratch + [pltpu.SemaphoreType.DMA((19,))],
    )(place, *sources, *weights)


def unproject(place, pieces, jobs_of, total, weights, rank_col):
    units, width = weights[0].shape
    wide = pieces[0].shape[-1]
    arrays = list(pieces)
    expand = rank_col is not None
    half = (rank_col.shape[0] if expand else total) // 2
    count = len(jobs_of(0, 0))

    def kernel(place_ref, *refs):
        ins, w_refs = refs[: len(arrays)], refs[len(arrays) : len(arrays) + 2]
        rest = refs[len(arrays) + 2 :]
        if expand:
            rank, rest = rest[0][...], rest[1:]
        outs, bufs, sems = rest[:4], rest[4:6], rest[6]
        jobs = [
            pltpu.make_async_copy(ins[i].at[src], outs[o].at[dst], sems.at[n])
            for n, (o, dst, i, src) in enumerate(jobs_of(place_ref[0], place_ref[1]))
        ]
        jobs += [pltpu.make_async_copy(w_refs[i], bufs[i], sems.at[count + i]) for i in (0, 1)]
        for job in jobs:
            job.start()
        for job in jobs:
            job.wait()
        if expand:
            part = (dot(outs[0][:, :units], bufs[0][...], (1, 0)) + dot(outs[1][:, :units], bufs[1][...], (1, 0))).astype(BF)
            pick = (rank == lax.broadcasted_iota(jnp.int32, (rank.shape[0], total), 1)).astype(F32).astype(BF)
            for n in (0, 1):
                outs[2 + n][...] = dot(pick[n * half : (n + 1) * half], part, (1, 0)).astype(BF)
        else:
            for n in (0, 1):
                rows = slice(n * half, (n + 1) * half)
                outs[2 + n][...] = (dot(outs[0][rows, :units], bufs[0][...], (1, 0)) + dot(outs[1][rows, :units], bufs[1][...], (1, 0))).astype(BF)

    anywhere = pl.BlockSpec(memory_space=pl.ANY)
    vmem = pl.BlockSpec(memory_space=pltpu.VMEM)
    shapes = [(total, wide)] * 2 + [(half, width)] * 2
    return pl.pallas_call(
        kernel,
        out_shape=[jax.ShapeDtypeStruct(s, BF) for s in shapes],
        in_specs=[pl.BlockSpec(memory_space=pltpu.SMEM)] + [anywhere] * (len(arrays) + 2) + [vmem] * expand,
        out_specs=[vmem] * 4,
        scratch_shapes=[pltpu.VMEM((units, width), BF)] * 2 + [pltpu.SemaphoreType.DMA((count + 2,))],
    )(place, *arrays, *weights, *([rank_col] if expand else []))


def over_y(blocks, step):
    return [blocks[0]] + [shift(blocks[k], "y", 4, step * k) for k in (1, 2, 3)]


def add(blocks):
    return sum(b.astype(F32) for b in blocks[1:]) + blocks[0].astype(F32)


def pack_rows(place, blocks):
    n, rows, width = blocks[0].shape
    return move(
        place, blocks, [(n, len(blocks) * rows, width)],
        lambda y, xl: [(0, (i, span(k * rows, rows)), k, (i, span(0, rows))) for k in range(len(blocks)) for i in range(n)],
    )[0]


def swiglu_back(totals):
    gate_sum, up_sum, back_sum = totals[0], totals[1], totals[2]
    sigmoid_gate = jax.nn.sigmoid(gate_sum)
    hidden = gate_sum * sigmoid_gate * up_sum
    d_gate = back_sum * up_sum * sigmoid_gate * (1.0 + gate_sum * (1.0 - sigmoid_gate))
    d_up = back_sum * gate_sum * sigmoid_gate
    return hidden.astype(BF), jnp.stack([d_gate.astype(BF), d_up.astype(BF)])


def pipeline(cap, place, rank, x0, g0, received0, mine_x, other_x, mine_g, other_g, w_gate, w_up, w_down, sums):
    r0, r1 = x0.shape[0] // 8, cap // 16
    weights = (w_gate, w_up, w_down)
    units = w_gate.shape[0]
    block = (rank % (8 * r1)) // r1
    dxl, dy = (block + place[1]) % 2, (block // 2 + 4 - place[0]) % 4
    at = jnp.where(rank >= 8 * r1, dy * 2 + dxl + 8, dxl * 4 + dy) * r1 + rank % r1
    rank = jnp.where(rank < 0, -1, at)

    def near_far(total, rows):
        return total[:, :rows], shift(total[:, rows:].astype(BF), "xl", 2, 1).astype(F32)

    halves = (mine_x, other_x, mine_g, other_g)
    xa, ga, near_a, far_a = project(place, (rank[None, :], *halves), weights, r1, False)
    far_a = shift(far_a, "xl", 2, 1)
    near0, far0 = near_far(add(after(xa, *received0)), r0)
    (rank_b,) = after(near0, rank)
    xb, gb, *parts_b = project(place, (rank_b[None, :] - 8 * r1, *halves), weights, r1, True)
    received_b = over_y(parts_b, 1)
    total_a = add(after(xb, near_a, far_a))
    received_a = over_y([total_a[:, :r1]] + [total_a[:, k * r1 : (k + 1) * r1].astype(BF) for k in (1, 2, 3)], 1)
    near_b, far_b = near_far(add(after(received_a[0], *received_b)), r1)
    near0, far0 = after(near_b, near0, far0)
    h0, s0 = swiglu_back(near0 + far0)
    swap_s0 = shift(s0, "xl", 2, 1)
    ha, sa = swiglu_back(add(after(s0, *received_a)))
    all_a = over_y([sa] * 4, -1)
    pair0 = pack_rows(place, after(sa, s0, swap_s0))
    near_b, far_b = after(pair0, near_b, far_b)
    hb, sb = swiglu_back(near_b + far_b)
    swap_b = shift(sb, "xl", 2, 1)
    h_all = jnp.concatenate([h0, ha, hb], axis=0)[None]
    swap_h = shift(h_all, "xl", 2, 1)
    pair_h = pack_rows(place, after(sb, h_all, swap_h))
    all_a = pack_rows(place, after(pair_h, *all_a))
    pieces_a = [all_a, shift(all_a, "xl", 2, 1)]
    pair_b = pack_rows(place, after(all_a, sb, swap_b))
    all_b = over_y([pair_b] * 4, -1)
    pieces0 = over_y([pair0] * 4, -1)
    all_h = over_y([pair_h] * 4, -1)

    def jobs0(y, xl):
        return [
            (i, span((((y + k) % 4) * 2 + (xl + d) % 2) * r0, r0), k, (i, span(d * r0, r0)))
            for d in (0, 1) for k in range(4) for i in (0, 1)
        ]

    def jobs1(y, xl):
        jobs = [(i, span(n * 4 * r1, 4 * r1), n, (i, span(0, 4 * r1))) for n in range(2) for i in (0, 1)]
        return jobs + [(i, span((8 + 2 * n) * r1, 2 * r1), 2 + n, (i, span(0, 2 * r1))) for n in range(4) for i in (0, 1)]

    dgd, dud, *halves = unproject(place, after(pair_b, *pieces0[1:], *pieces_a, *all_b)[3:], jobs1, cap, weights[:2], rank[:, None])
    swap1 = shift(halves[1], "c", 2, 1)
    dg0, du0, *halves0 = unproject(place, after(dgd, *pieces0), jobs0, 8 * r0, weights[:2], None)
    swap0 = shift(halves0[1], "c", 2, 1)
    xd, gd = jnp.concatenate([xa, xb], axis=0), jnp.concatenate([ga, gb], axis=0)

    def outer(total, first, late, other_first, other_late):
        return (total + dot(first[:, :units], other_first, (0, 0)) + dot(late[:, :units], other_late, (0, 0))).astype(BF)

    rows0, rows1, width = r0 // 2, halves[0].shape[0] // 8, x0.shape[1]
    own1, swap1 = after(dg0, halves[0], swap1)
    total1 = (own1.astype(F32) + swap1.astype(F32)).reshape(2, 4, rows1, width)
    left, right = total1[..., : width // 2], total1[..., width // 2 :]
    far_left = shift(left[1].astype(BF), "xh", 2, 1)
    far_right = [shift(right[:, k].astype(BF), "z", 4, k) for k in (1, 2, 3)]
    (xd_late,) = after(total1, xd)
    grad_gate = outer(sums[2], dg0, dgd, x0, xd_late)
    own0, swap0, far_left, *far_right = after(grad_gate, halves0[0], swap0, far_left, *far_right)
    total0 = own0.astype(F32) + swap0.astype(F32)
    far0 = shift(total0[4 * rows0 :].astype(BF), "xh", 2, 1)
    left = left[0] + far_left.astype(F32)
    right = right[:, 0] + sum(f.astype(F32) for f in far_right)
    far_left = [shift(left[k].astype(BF), "z", 4, k) for k in (1, 2, 3)]
    far_right = shift(right[1].astype(BF), "xh", 2, 1)
    (xd_late,) = after((left[0] + right[0]).astype(BF), xd_late)
    grad_up = outer(sums[3], du0, dud, x0, xd_late)
    far0, far_right, *far_left = after(grad_up, far0, far_right, *far_left)
    total0 = total0[: 4 * rows0] + far0.astype(F32)
    out0 = total0[:rows0] + sum(shift(total0[k * rows0 : (k + 1) * rows0].astype(BF), "z", 4, k).astype(F32) for k in (1, 2, 3))
    out1 = jnp.concatenate([left[0] + sum(f.astype(F32) for f in far_left), right[0] + far_right.astype(F32)], axis=1)
    pieces = after(grad_up, *all_h)
    total = r0 + 2 * r1

    def copies(y, xl):
        jobs = []
        for k in range(4):
            for d in (0, 1):
                here = ((y + k) % 4) * 2 + (xl + d) % 2
                low = d * total
                jobs.append((0, span(here * r0, r0), k, (0, span(low, r0))))
                jobs.append((1, span((4 * d + k) * r1, r1), k, (0, span(low + r0, r1))))
                jobs.append((1, span((8 + 2 * k + d) * r1, r1), k, (0, span(low + r0 + r1, r1))))
        return jobs

    hidden0, hidden_d = move(place, pieces, [(8 * r0, h0.shape[1]), (cap, h0.shape[1])], copies)
    grad_down = outer(sums[4], hidden0, hidden_d, g0, gd)
    return (sums[0] + out0).astype(BF), (sums[1] + out1).astype(BF), grad_gate, grad_up, grad_down


def shards(activations, output_grad, tile_counts, w_gate, w_up, w_down):
    own_rows, width = activations.shape
    tiles, n_tiles = own_rows // TILE, tile_counts.shape[0]
    tail = TILE - HEAD
    y, xl = lax.axis_index("y"), lax.axis_index("xl")
    xh, z, c = lax.axis_index("xh"), lax.axis_index("z"), lax.axis_index("c")
    place = jnp.stack([y, xl]).astype(jnp.int32)
    live = jnp.sum(tile_counts) - HEAD * n_tiles

    w_gate, w_up = w_gate.T, w_up.T

    def one_pass(state):
        step, sums = state
        sums = [jnp.where(step > 0, value.astype(F32), 0.0) for value in sums]
        acts = activations.reshape(tiles, TILE, width)
        grads = output_grad.reshape(tiles, TILE, width)
        first = (step == 0).astype(BF) * jnp.concatenate([acts[:, :HEAD].reshape(-1, width), grads[:, :HEAD].reshape(-1, width)], axis=0)
        rows = tiles * HEAD
        far = shift(first, "xh", 2, 1)
        pair = join(place, [first, far])
        late_x, late_g = acts[:, HEAD:].reshape(-1, width), grads[:, HEAD:].reshape(-1, width)
        late_x, late_g = after(pair, late_x, late_g)
        moved_x = over_z(late_x)
        far_g = shift(late_g, "xh", 2, 1)
        mine = by_core(place, over_z(pair), 2 * rows)
        other = shift(mine, "c", 2, 1)
        pair_g = join(place, after(mine, late_g, far_g))
        moved_g = over_z(pair_g)
        mine, other = after(pair_g, mine, other)
        x0, g0 = move(
            place, [mine, other], [(16 * rows, width)] * 2,
            lambda y, xl: [(i, span((8 * d + n) * rows, rows), d, span((2 * n + i) * rows, rows)) for d in (0, 1) for n in range(8) for i in (0, 1)],
        )
        near_x = join(place, after(x0, *moved_x))
        far_x = shift(near_x, "xh", 2, 1)
        parts0 = project(place, after(near_x, x0, g0), (w_gate, w_up, w_down), x0.shape[0] // 8, True)
        received0 = over_y(parts0, 1)
        mine_g = by_core(place, after(parts0[0], received0[1], received0[3], *moved_g)[2:], late_x.shape[0])
        mine_x = join(place, after(mine_g, near_x, far_x))
        halves = (mine_x, shift(mine_x, "c", 2, 1), mine_g, shift(mine_g, "c", 2, 1))
        order = lax.iota(jnp.int32, n_tiles)
        dev, sub = order // tiles, order % tiles
        source = (((xh + (dev // 4) % 2) % 2) * 4 + (z + dev % 4) % 4) * 2 + (c + dev // 8) % 2
        wanted = source * tiles + sub
        counts = jnp.sum(jnp.where(wanted[:, None] == order[None, :], tile_counts[None, :], 0), axis=1)
        extra = counts - HEAD
        before = jnp.sum(jnp.where(order[None, :] < order[:, None], extra[None, :], 0), axis=1)
        slot = lax.iota(jnp.int32, tail)
        rank = jnp.where(slot[None, :] < extra[:, None], before[:, None] + slot[None, :], -1).reshape(-1)
        here = rank - step * CAP
        here = jnp.where((rank >= 0) & (here >= 0) & (here < CAP), here, -1)
        results = pipeline(CAP, place, here, x0, g0, received0, *halves, w_gate, w_up, w_down, sums)
        return step + 1, results

    rows = tiles * HEAD
    shapes = ((rows, width), (own_rows - rows, width), w_gate.shape, w_up.shape, w_down.shape)
    start = (jnp.int32(0), tuple(blank(shapes)))
    _, sums = lax.while_loop(lambda state: state[0] * CAP < jnp.maximum(live, 1), one_pass, start)
    out0, out1, grad_gate, grad_up, grad_down = sums
    input_grad = jnp.concatenate([out0.reshape(tiles, HEAD, width), out1.reshape(tiles, tail, width)], axis=1)
    return (input_grad.reshape(own_rows, width), grad_gate.T, grad_up.T, grad_down)


def solution(mesh):
    fine = Mesh(mesh.devices.reshape(4, 2, 2, 4, 2), ("y", "xl", "xh", "z", "c"))
    row, col = ("y", "xl"), ("xh", "z", "c")
    in_specs = (P(col, row), P(col, row), P(), P(row, col), P(row, col), P(col, row))
    out_specs = (P(col, row), P(row, col), P(row, col), P(col, row))
    return jax.shard_map(shards, mesh=fine, in_specs=in_specs, out_specs=out_specs, check_vma=False)
```

```python
import jax
import jax.numpy as jnp
from jax import lax
from jax.experimental import pallas as pl
from jax.experimental.pallas import tpu as pltpu
from jax.sharding import Mesh, PartitionSpec as P

TILE = 64
HEAD = 16
CAP = 1024
BF = jnp.bfloat16
F32 = jnp.float32


def dot(left, right, dims):
    return lax.dot_general(left, right, ((dims[:1], dims[1:]), ((), ())), preferred_element_type=F32)


def shift(value, axis, size, step):
    return lax.ppermute(value, axis, [(i, (i + step) % size) for i in range(size)])


def move(place, sources, shapes, copies):
    count = len(copies(0, 0))

    def kernel(place_ref, *refs):
        ins, outs, sems = refs[: len(sources)], refs[len(sources) : -1], refs[-1]
        jobs = [
            pltpu.make_async_copy(ins[i].at[src], outs[o].at[dst], sems.at[n])
            for n, (o, dst, i, src) in enumerate(copies(place_ref[0], place_ref[1]))
        ]
        for job in jobs:
            job.start()
        for job in jobs:
            job.wait()

    anywhere = pl.BlockSpec(memory_space=pl.ANY)
    return pl.pallas_call(
        kernel,
        out_shape=[jax.ShapeDtypeStruct(s, BF) for s in shapes],
        in_specs=[pl.BlockSpec(memory_space=pltpu.SMEM)] + [anywhere] * len(sources),
        out_specs=[pl.BlockSpec(memory_space=pltpu.VMEM)] * len(shapes),
        scratch_shapes=[pltpu.SemaphoreType.DMA((count,))],
    )(place, *sources)


def after(token, *values):
    return lax.optimization_barrier((*values, token))[:-1]


def blank(shapes):
    return pl.pallas_call(
        lambda *refs: None,
        out_shape=[jax.ShapeDtypeStruct(s, BF) for s in shapes],
        out_specs=[pl.BlockSpec(memory_space=pl.ANY)] * len(shapes),
    )()


def span(start, size):
    return pl.ds(start if isinstance(start, int) else pl.multiple_of(start, 8), size)


def join(place, blocks):
    rows, width = blocks[0].shape
    return move(place, blocks, [(len(blocks) * rows, width)], lambda y, xl: [(0, span(n * rows, rows), n, span(0, rows)) for n in range(len(blocks))])[0]


def by_core(place, moved, rows):
    return move(
        place, moved, [(8 * rows, moved[0].shape[1])],
        lambda y, xl: [(0, span((4 * d + n) * rows, rows), n, span(d * rows, rows)) for n in range(4) for d in (0, 1)],
    )[0]


def over_z(value):
    return [value] + [shift(value, "z", 4, -k) for k in (1, 2, 3)]


def project(place, sources, weights, rows, y_first):
    units, width = weights[0].shape
    wide = -(-units // 128) * 128
    compact = len(sources) > 2
    total = 8 * rows
    if y_first:
        cuts = [(k * 2 * rows, 2 * rows) for k in range(4)]
    else:
        cuts = [(n * 4 * rows, 4 * rows) for n in range(2)]
    shapes = [(3, size, wide) for _, size in cuts]
    if compact:
        shapes = [(total, width)] * 2 + shapes
    n_in = len(sources) + 3

    def kernel(place_ref, *refs):
        ins, w_refs, outs = refs[: len(sources)], refs[len(sources) : n_in], refs[n_in : n_in + len(shapes)]
        bufs, sems = refs[n_in + len(shapes) : -1], refs[-1]
        jobs = []

        def start(src, dst):
            job = pltpu.make_async_copy(src, dst, sems.at[len(jobs)])
            job.start()
            jobs.append(job)
            return job

        if compact:
            rank = ins[0][...]
            feeds = [start(ins[1 + i], bufs[3 + i]) for i in range(4)]
        else:
            feeds = []
            for i in (0, 1):
                for k in range(4):
                    for d in (0, 1):
                        block = ((place_ref[0] + k) % 4) * 2 + (place_ref[1] + d) % 2
                        feeds.append(start(ins[i].at[span(block * rows, rows)], bufs[3 + i].at[span((2 * k + d) * rows, rows)]))
        loads = [start(w_refs[i], bufs[i]) for i in range(3)]
        if compact:
            pick = (lax.broadcasted_iota(jnp.int32, (total, rank.shape[1]), 0) == rank).astype(F32).astype(BF)
            half = rank.shape[1] // 2
            for i in (0, 1):
                feeds[2 * i].wait()
                feeds[2 * i + 1].wait()
                outs[i][...] = (dot(pick[:, :half], bufs[3 + 2 * i][...], (1, 0)) + dot(pick[:, half:], bufs[4 + 2 * i][...], (1, 0))).astype(BF)
            lefts = outs[:2]
            packs = outs[2:]
        else:
            for feed in feeds:
                feed.wait()
            lefts = bufs[3:5]
            packs = outs
        for i in range(3):
            loads[i].wait()
            for (low, size), out in zip(cuts, packs):
                left = lefts[i // 2][low : low + size]
                out[i, :, :units] = dot(left, bufs[i][...], (1, 1)).astype(BF)
                out[i, :, units:] = jnp.zeros((size, wide - units), BF)

    anywhere = pl.BlockSpec(memory_space=pl.ANY)
    vmem = pl.BlockSpec(memory_space=pltpu.VMEM)
    smem = pl.BlockSpec(memory_space=pltpu.SMEM)
    scratch = [pltpu.VMEM(w.shape, BF) for w in weights]
    scratch += [pltpu.VMEM(s.shape, BF) for s in (sources[1:] if compact else sources)]
    return pl.pallas_call(
        kernel,
        out_shape=[jax.ShapeDtypeStruct(s, BF) for s in shapes],
        in_specs=[smem] + ([vmem] if compact else []) + [anywhere] * (n_in - compact),
        out_specs=[vmem] * len(shapes),
        scratch_shapes=scratch + [pltpu.SemaphoreType.DMA((19,))],
    )(place, *sources, *weights)


def unproject(place, pieces, jobs_of, total, weights, rank_col):
    units, width = weights[0].shape
    wide = pieces[0].shape[-1]
    arrays = list(pieces)
    expand = rank_col is not None
    half = (rank_col.shape[0] if expand else total) // 2
    count = len(jobs_of(0, 0))

    def kernel(place_ref, *refs):
        ins, w_refs = refs[: len(arrays)], refs[len(arrays) : len(arrays) + 2]
        rest = refs[len(arrays) + 2 :]
        if expand:
            rank, rest = rest[0][...], rest[1:]
        outs, bufs, sems = rest[:4], rest[4:6], rest[6]
        jobs = [
            pltpu.make_async_copy(ins[i].at[src], outs[o].at[dst], sems.at[n])
            for n, (o, dst, i, src) in enumerate(jobs_of(place_ref[0], place_ref[1]))
        ]
        jobs += [pltpu.make_async_copy(w_refs[i], bufs[i], sems.at[count + i]) for i in (0, 1)]
        for job in jobs:
            job.start()
        for job in jobs:
            job.wait()
        if expand:
            part = (dot(outs[0][:, :units], bufs[0][...], (1, 0)) + dot(outs[1][:, :units], bufs[1][...], (1, 0))).astype(BF)
            pick = (rank == lax.broadcasted_iota(jnp.int32, (rank.shape[0], total), 1)).astype(F32).astype(BF)
            for n in (0, 1):
                outs[2 + n][...] = dot(pick[n * half : (n + 1) * half], part, (1, 0)).astype(BF)
        else:
            for n in (0, 1):
                rows = slice(n * half, (n + 1) * half)
                outs[2 + n][...] = (dot(outs[0][rows, :units], bufs[0][...], (1, 0)) + dot(outs[1][rows, :units], bufs[1][...], (1, 0))).astype(BF)

    anywhere = pl.BlockSpec(memory_space=pl.ANY)
    vmem = pl.BlockSpec(memory_space=pltpu.VMEM)
    shapes = [(total, wide)] * 2 + [(half, width)] * 2
    return pl.pallas_call(
        kernel,
        out_shape=[jax.ShapeDtypeStruct(s, BF) for s in shapes],
        in_specs=[pl.BlockSpec(memory_space=pltpu.SMEM)] + [anywhere] * (len(arrays) + 2) + [vmem] * expand,
        out_specs=[vmem] * 4,
        scratch_shapes=[pltpu.VMEM((units, width), BF)] * 2 + [pltpu.SemaphoreType.DMA((count + 2,))],
    )(place, *arrays, *weights, *([rank_col] if expand else []))


def over_y(blocks, step):
    return [blocks[0]] + [shift(blocks[k], "y", 4, step * k) for k in (1, 2, 3)]


def add(blocks):
    return sum(b.astype(F32) for b in blocks[1:]) + blocks[0].astype(F32)


def pack_rows(place, blocks):
    n, rows, width = blocks[0].shape
    return move(
        place, blocks, [(n, len(blocks) * rows, width)],
        lambda y, xl: [(0, (i, span(k * rows, rows)), k, (i, span(0, rows))) for k in range(len(blocks)) for i in range(n)],
    )[0]


def swiglu_back(totals):
    gate_sum, up_sum, back_sum = totals[0], totals[1], totals[2]
    sigmoid_gate = jax.nn.sigmoid(gate_sum)
    hidden = gate_sum * sigmoid_gate * up_sum
    d_gate = back_sum * up_sum * sigmoid_gate * (1.0 + gate_sum * (1.0 - sigmoid_gate))
    d_up = back_sum * gate_sum * sigmoid_gate
    return hidden.astype(BF), jnp.stack([d_gate.astype(BF), d_up.astype(BF)])


def pipeline(cap, place, rank, x0, g0, received0, mine_x, other_x, mine_g, other_g, w_gate, w_up, w_down, sums):
    r0, r1 = x0.shape[0] // 8, cap // 16
    weights = (w_gate, w_up, w_down)
    units = w_gate.shape[0]
    block = (rank % (8 * r1)) // r1
    dxl, dy = (block + place[1]) % 2, (block // 2 + 4 - place[0]) % 4
    at = jnp.where(rank >= 8 * r1, dy * 2 + dxl + 8, dxl * 4 + dy) * r1 + rank % r1
    rank = jnp.where(rank < 0, -1, at)

    def near_far(total, rows):
        return total[:, :rows], shift(total[:, rows:].astype(BF), "xl", 2, 1).astype(F32)

    halves = (mine_x, other_x, mine_g, other_g)
    xa, ga, near_a, far_a = project(place, (rank[None, :], *halves), weights, r1, False)
    far_a = shift(far_a, "xl", 2, 1)
    near0, far0 = near_far(add(after(xa, *received0)), r0)
    (rank_b,) = after(near0, rank)
    xb, gb, *parts_b = project(place, (rank_b[None, :] - 8 * r1, *halves), weights, r1, True)
    received_b = over_y(parts_b, 1)
    total_a = add(after(xb, near_a, far_a))
    received_a = over_y([total_a[:, :r1]] + [total_a[:, k * r1 : (k + 1) * r1].astype(BF) for k in (1, 2, 3)], 1)
    near_b, far_b = near_far(add(after(received_a[0], *received_b)), r1)
    near0, far0 = after(near_b, near0, far0)
    h0, s0 = swiglu_back(near0 + far0)
    swap_s0 = shift(s0, "xl", 2, 1)
    ha, sa = swiglu_back(add(after(s0, *received_a)))
    all_a = over_y([sa] * 4, -1)
    pair0 = pack_rows(place, after(sa, s0, swap_s0))
    near_b, far_b = after(pair0, near_b, far_b)
    hb, sb = swiglu_back(near_b + far_b)
    swap_b = shift(sb, "xl", 2, 1)
    h_all = jnp.concatenate([h0, ha, hb], axis=0)[None]
    swap_h = shift(h_all, "xl", 2, 1)
    pair_h = pack_rows(place, after(sb, h_all, swap_h))
    all_a = pack_rows(place, after(pair_h, *all_a))
    pieces_a = [all_a, shift(all_a, "xl", 2, 1)]
    pair_b = pack_rows(place, after(all_a, sb, swap_b))
    all_b = over_y([pair_b] * 4, -1)
    pieces0 = over_y([pair0] * 4, -1)
    all_h = over_y([pair_h] * 4, -1)

    def jobs0(y, xl):
        return [
            (i, span((((y + k) % 4) * 2 + (xl + d) % 2) * r0, r0), k, (i, span(d * r0, r0)))
            for d in (0, 1) for k in range(4) for i in (0, 1)
        ]

    def jobs1(y, xl):
        jobs = [(i, span(n * 4 * r1, 4 * r1), n, (i, span(0, 4 * r1))) for n in range(2) for i in (0, 1)]
        return jobs + [(i, span((8 + 2 * n) * r1, 2 * r1), 2 + n, (i, span(0, 2 * r1))) for n in range(4) for i in (0, 1)]

    dgd, dud, *halves = unproject(place, after(pair_b, *pieces0[1:], *pieces_a, *all_b)[3:], jobs1, cap, weights[:2], rank[:, None])
    swap1 = shift(halves[1], "c", 2, 1)
    dg0, du0, *halves0 = unproject(place, after(dgd, *pieces0), jobs0, 8 * r0, weights[:2], None)
    swap0 = shift(halves0[1], "c", 2, 1)
    xd, gd = jnp.concatenate([xa, xb], axis=0), jnp.concatenate([ga, gb], axis=0)

    def outer(total, first, late, other_first, other_late):
        return (total + dot(first[:, :units], other_first, (0, 0)) + dot(late[:, :units], other_late, (0, 0))).astype(BF)

    rows0, rows1, width = r0 // 2, halves[0].shape[0] // 8, x0.shape[1]
    own1, swap1 = after(dg0, halves[0], swap1)
    total1 = (own1.astype(F32) + swap1.astype(F32)).reshape(2, 4, rows1, width)
    left, right = total1[..., : width // 2], total1[..., width // 2 :]
    far_left = shift(left[1].astype(BF), "xh", 2, 1)
    far_right = [shift(right[:, k].astype(BF), "z", 4, k) for k in (1, 2, 3)]
    (xd_late,) = after(total1, xd)
    grad_gate = outer(sums[2], dg0, dgd, x0, xd_late)
    own0, swap0, far_left, *far_right = after(grad_gate, halves0[0], swap0, far_left, *far_right)
    total0 = own0.astype(F32) + swap0.astype(F32)
    far0 = shift(total0[4 * rows0 :].astype(BF), "xh", 2, 1)
    left = left[0] + far_left.astype(F32)
    right = right[:, 0] + sum(f.astype(F32) for f in far_right)
    far_left = [shift(left[k].astype(BF), "z", 4, k) for k in (1, 2, 3)]
    far_right = shift(right[1].astype(BF), "xh", 2, 1)
    (xd_late,) = after((left[0] + right[0]).astype(BF), xd_late)
    grad_up = outer(sums[3], du0, dud, x0, xd_late)
    far0, far_right, *far_left = after(grad_up, far0, far_right, *far_left)
    total0 = total0[: 4 * rows0] + far0.astype(F32)
    out0 = total0[:rows0] + sum(shift(total0[k * rows0 : (k + 1) * rows0].astype(BF), "z", 4, k).astype(F32) for k in (1, 2, 3))
    out1 = jnp.concatenate([left[0] + sum(f.astype(F32) for f in far_left), right[0] + far_right.astype(F32)], axis=1)
    pieces = after(total0.astype(BF), *all_h)
    total = r0 + 2 * r1

    def copies(y, xl):
        jobs = []
        for k in range(4):
            for d in (0, 1):
                here = ((y + k) % 4) * 2 + (xl + d) % 2
                low = d * total
                jobs.append((0, span(here * r0, r0), k, (0, span(low, r0))))
                jobs.append((1, span((4 * d + k) * r1, r1), k, (0, span(low + r0, r1))))
                jobs.append((1, span((8 + 2 * k + d) * r1, r1), k, (0, span(low + r0 + r1, r1))))
        return jobs

    hidden0, hidden_d = move(place, pieces, [(8 * r0, h0.shape[1]), (cap, h0.shape[1])], copies)
    grad_down = outer(sums[4], hidden0, hidden_d, g0, gd)
    return (sums[0] + out0).astype(BF), (sums[1] + out1).astype(BF), grad_gate, grad_up, grad_down


def shards(activations, output_grad, tile_counts, w_gate, w_up, w_down):
    own_rows, width = activations.shape
    tiles, n_tiles = own_rows // TILE, tile_counts.shape[0]
    tail = TILE - HEAD
    y, xl = lax.axis_index("y"), lax.axis_index("xl")
    xh, z, c = lax.axis_index("xh"), lax.axis_index("z"), lax.axis_index("c")
    place = jnp.stack([y, xl]).astype(jnp.int32)
    live = jnp.sum(tile_counts) - HEAD * n_tiles

    w_gate, w_up = w_gate.T, w_up.T

    def one_pass(state):
        step, sums = state
        sums = [jnp.where(step > 0, value.astype(F32), 0.0) for value in sums]
        acts = activations.reshape(tiles, TILE, width)
        grads = output_grad.reshape(tiles, TILE, width)
        first = (step == 0).astype(BF) * jnp.concatenate([acts[:, :HEAD].reshape(-1, width), grads[:, :HEAD].reshape(-1, width)], axis=0)
        rows = tiles * HEAD
        far = shift(first, "xh", 2, 1)
        pair = join(place, [first, far])
        late_x, late_g = acts[:, HEAD:].reshape(-1, width), grads[:, HEAD:].reshape(-1, width)
        late_x, late_g = after(pair, late_x, late_g)
        moved_x = over_z(late_x)
        far_g = shift(late_g, "xh", 2, 1)
        mine = by_core(place, over_z(pair), 2 * rows)
        other = shift(mine, "c", 2, 1)
        pair_g = join(place, after(mine, late_g, far_g))
        moved_g = over_z(pair_g)
        mine, other = after(pair_g, mine, other)
        x0, g0 = move(
            place, [mine, other], [(16 * rows, width)] * 2,
            lambda y, xl: [(i, span((8 * d + n) * rows, rows), d, span((2 * n + i) * rows, rows)) for d in (0, 1) for n in range(8) for i in (0, 1)],
        )
        near_x = join(place, after(x0, *moved_x))
        far_x = shift(near_x, "xh", 2, 1)
        parts0 = project(place, after(near_x, x0, g0), (w_gate, w_up, w_down), x0.shape[0] // 8, True)
        received0 = over_y(parts0, 1)
        mine_g = by_core(place, after(parts0[0], received0[1], received0[3], *moved_g)[2:], late_x.shape[0])
        mine_x = join(place, after(mine_g, near_x, far_x))
        halves = (mine_x, shift(mine_x, "c", 2, 1), mine_g, shift(mine_g, "c", 2, 1))
        order = lax.iota(jnp.int32, n_tiles)
        dev, sub = order // tiles, order % tiles
        source = (((xh + (dev // 4) % 2) % 2) * 4 + (z + dev % 4) % 4) * 2 + (c + dev // 8) % 2
        wanted = source * tiles + sub
        counts = jnp.sum(jnp.where(wanted[:, None] == order[None, :], tile_counts[None, :], 0), axis=1)
        extra = counts - HEAD
        before = jnp.sum(jnp.where(order[None, :] < order[:, None], extra[None, :], 0), axis=1)
        slot = lax.iota(jnp.int32, tail)
        rank = jnp.where(slot[None, :] < extra[:, None], before[:, None] + slot[None, :], -1).reshape(-1)
        here = rank - step * CAP
        here = jnp.where((rank >= 0) & (here >= 0) & (here < CAP), here, -1)
        results = pipeline(CAP, place, here, x0, g0, received0, *halves, w_gate, w_up, w_down, sums)
        return step + 1, results

    rows = tiles * HEAD
    shapes = ((rows, width), (own_rows - rows, width), w_gate.shape, w_up.shape, w_down.shape)
    start = (jnp.int32(0), tuple(blank(shapes)))
    _, sums = lax.while_loop(lambda state: state[0] * CAP < jnp.maximum(live, 1), one_pass, start)
    out0, out1, grad_gate, grad_up, grad_down = sums
    input_grad = jnp.concatenate([out0.reshape(tiles, HEAD, width), out1.reshape(tiles, tail, width)], axis=1)
    return (input_grad.reshape(own_rows, width), grad_gate.T, grad_up.T, grad_down)


def solution(mesh):
    fine = Mesh(mesh.devices.reshape(4, 2, 2, 4, 2), ("y", "xl", "xh", "z", "c"))
    row, col = ("y", "xl"), ("xh", "z", "c")
    in_specs = (P(col, row), P(col, row), P(), P(row, col), P(row, col), P(col, row))
    out_specs = (P(col, row), P(row, col), P(row, col), P(col, row))
    return jax.shard_map(shards, mesh=fine, in_specs=in_specs, out_specs=out_specs, check_vma=False)
```

```python
import jax
import jax.numpy as jnp
from jax import lax
from jax.experimental import pallas as pl
from jax.experimental.pallas import tpu as pltpu
from jax.sharding import Mesh, PartitionSpec as P

TILE = 64
HEAD = 16
CAP = 1024
BF = jnp.bfloat16
F32 = jnp.float32


def dot(left, right, dims):
    return lax.dot_general(left, right, ((dims[:1], dims[1:]), ((), ())), preferred_element_type=F32)


def shift(value, axis, size, step):
    return lax.ppermute(value, axis, [(i, (i + step) % size) for i in range(size)])


def move(place, sources, shapes, copies):
    count = len(copies(0, 0))

    def kernel(place_ref, *refs):
        ins, outs, sems = refs[: len(sources)], refs[len(sources) : -1], refs[-1]
        jobs = [
            pltpu.make_async_copy(ins[i].at[src], outs[o].at[dst], sems.at[n])
            for n, (o, dst, i, src) in enumerate(copies(place_ref[0], place_ref[1]))
        ]
        for job in jobs:
            job.start()
        for job in jobs:
            job.wait()

    anywhere = pl.BlockSpec(memory_space=pl.ANY)
    return pl.pallas_call(
        kernel,
        out_shape=[jax.ShapeDtypeStruct(s, BF) for s in shapes],
        in_specs=[pl.BlockSpec(memory_space=pltpu.SMEM)] + [anywhere] * len(sources),
        out_specs=[pl.BlockSpec(memory_space=pltpu.VMEM)] * len(shapes),
        scratch_shapes=[pltpu.SemaphoreType.DMA((count,))],
    )(place, *sources)


def after(token, *values):
    return lax.optimization_barrier((*values, token))[:-1]


def blank(shapes):
    return pl.pallas_call(
        lambda *refs: None,
        out_shape=[jax.ShapeDtypeStruct(s, BF) for s in shapes],
        out_specs=[pl.BlockSpec(memory_space=pl.ANY)] * len(shapes),
    )()


def span(start, size):
    return pl.ds(start if isinstance(start, int) else pl.multiple_of(start, 8), size)


def join(place, blocks):
    rows, width = blocks[0].shape
    return move(place, blocks, [(len(blocks) * rows, width)], lambda y, xl: [(0, span(n * rows, rows), n, span(0, rows)) for n in range(len(blocks))])[0]


def by_core(place, moved, rows):
    return move(
        place, moved, [(8 * rows, moved[0].shape[1])],
        lambda y, xl: [(0, span((4 * d + n) * rows, rows), n, span(d * rows, rows)) for n in range(4) for d in (0, 1)],
    )[0]


def over_z(value):
    return [value] + [shift(value, "z", 4, -k) for k in (1, 2, 3)]


def project(place, sources, weights, rows, y_first):
    units, width = weights[0].shape
    wide = -(-units // 128) * 128
    compact = len(sources) > 2
    total = 8 * rows
    if y_first:
        cuts = [(k * 2 * rows, 2 * rows) for k in range(4)]
    else:
        cuts = [(n * 4 * rows, 4 * rows) for n in range(2)]
    shapes = [(3, size, wide) for _, size in cuts]
    if compact:
        shapes = [(total, width)] * 2 + shapes
    n_in = len(sources) + 3

    def kernel(place_ref, *refs):
        ins, w_refs, outs = refs[: len(sources)], refs[len(sources) : n_in], refs[n_in : n_in + len(shapes)]
        bufs, sems = refs[n_in + len(shapes) : -1], refs[-1]
        jobs = []

        def start(src, dst):
            job = pltpu.make_async_copy(src, dst, sems.at[len(jobs)])
            job.start()
            jobs.append(job)
            return job

        if compact:
            rank = ins[0][...]
            feeds = [start(ins[1 + i], bufs[3 + i]) for i in range(4)]
        else:
            feeds = []
            for i in (0, 1):
                for k in range(4):
                    for d in (0, 1):
                        block = ((place_ref[0] + k) % 4) * 2 + (place_ref[1] + d) % 2
                        feeds.append(start(ins[i].at[span(block * rows, rows)], bufs[3 + i].at[span((2 * k + d if y_first else 4 * d + k) * rows, rows)]))
        loads = [start(w_refs[i], bufs[i]) for i in range(3)]
        if compact:
            pick = (lax.broadcasted_iota(jnp.int32, (total, rank.shape[1]), 0) == rank).astype(F32).astype(BF)
            half = rank.shape[1] // 2
            for i in (0, 1):
                feeds[2 * i].wait()
                feeds[2 * i + 1].wait()
                outs[i][...] = (dot(pick[:, :half], bufs[3 + 2 * i][...], (1, 0)) + dot(pick[:, half:], bufs[4 + 2 * i][...], (1, 0))).astype(BF)
            lefts = outs[:2]
            packs = outs[2:]
        else:
            for feed in feeds:
                feed.wait()
            lefts = bufs[3:5]
            packs = outs
        for i in range(3):
            loads[i].wait()
            for (low, size), out in zip(cuts, packs):
                left = lefts[i // 2][low : low + size]
                out[i, :, :units] = dot(left, bufs[i][...], (1, 1)).astype(BF)
                out[i, :, units:] = jnp.zeros((size, wide - units), BF)

    anywhere = pl.BlockSpec(memory_space=pl.ANY)
    vmem = pl.BlockSpec(memory_space=pltpu.VMEM)
    smem = pl.BlockSpec(memory_space=pltpu.SMEM)
    scratch = [pltpu.VMEM(w.shape, BF) for w in weights]
    scratch += [pltpu.VMEM(s.shape, BF) for s in (sources[1:] if compact else sources)]
    return pl.pallas_call(
        kernel,
        out_shape=[jax.ShapeDtypeStruct(s, BF) for s in shapes],
        in_specs=[smem] + ([vmem] if compact else []) + [anywhere] * (n_in - compact),
        out_specs=[vmem] * len(shapes),
        scratch_shapes=scratch + [pltpu.SemaphoreType.DMA((19,))],
    )(place, *sources, *weights)


def unproject(place, pieces, jobs_of, total, weights, rank_col):
    units, width = weights[0].shape
    wide = pieces[0].shape[-1]
    arrays = list(pieces)
    expand = rank_col is not None
    half = (rank_col.shape[0] if expand else total) // 2
    count = len(jobs_of(0, 0))

    def kernel(place_ref, *refs):
        ins, w_refs = refs[: len(arrays)], refs[len(arrays) : len(arrays) + 2]
        rest = refs[len(arrays) + 2 :]
        if expand:
            rank, rest = rest[0][...], rest[1:]
        outs, bufs, sems = rest[:4], rest[4:6], rest[6]
        jobs = [
            pltpu.make_async_copy(ins[i].at[src], outs[o].at[dst], sems.at[n])
            for n, (o, dst, i, src) in enumerate(jobs_of(place_ref[0], place_ref[1]))
        ]
        jobs += [pltpu.make_async_copy(w_refs[i], bufs[i], sems.at[count + i]) for i in (0, 1)]
        for job in jobs:
            job.start()
        for job in jobs:
            job.wait()
        if expand:
            part = (dot(outs[0][:, :units], bufs[0][...], (1, 0)) + dot(outs[1][:, :units], bufs[1][...], (1, 0))).astype(BF)
            pick = (rank == lax.broadcasted_iota(jnp.int32, (rank.shape[0], total), 1)).astype(F32).astype(BF)
            for n in (0, 1):
                outs[2 + n][...] = dot(pick[n * half : (n + 1) * half], part, (1, 0)).astype(BF)
        else:
            for n in (0, 1):
                rows = slice(n * half, (n + 1) * half)
                outs[2 + n][...] = (dot(outs[0][rows, :units], bufs[0][...], (1, 0)) + dot(outs[1][rows, :units], bufs[1][...], (1, 0))).astype(BF)

    anywhere = pl.BlockSpec(memory_space=pl.ANY)
    vmem = pl.BlockSpec(memory_space=pltpu.VMEM)
    shapes = [(total, wide)] * 2 + [(half, width)] * 2
    return pl.pallas_call(
        kernel,
        out_shape=[jax.ShapeDtypeStruct(s, BF) for s in shapes],
        in_specs=[pl.BlockSpec(memory_space=pltpu.SMEM)] + [anywhere] * (len(arrays) + 2) + [vmem] * expand,
        out_specs=[vmem] * 4,
        scratch_shapes=[pltpu.VMEM((units, width), BF)] * 2 + [pltpu.SemaphoreType.DMA((count + 2,))],
    )(place, *arrays, *weights, *([rank_col] if expand else []))


def over_y(blocks, step):
    return [blocks[0]] + [shift(blocks[k], "y", 4, step * k) for k in (1, 2, 3)]


def add(blocks):
    return sum(b.astype(F32) for b in blocks[1:]) + blocks[0].astype(F32)


def pack_rows(place, blocks):
    n, rows, width = blocks[0].shape
    return move(
        place, blocks, [(n, len(blocks) * rows, width)],
        lambda y, xl: [(0, (i, span(k * rows, rows)), k, (i, span(0, rows))) for k in range(len(blocks)) for i in range(n)],
    )[0]


def swiglu_back(totals):
    gate_sum, up_sum, back_sum = totals[0], totals[1], totals[2]
    sigmoid_gate = jax.nn.sigmoid(gate_sum)
    hidden = gate_sum * sigmoid_gate * up_sum
    d_gate = back_sum * up_sum * sigmoid_gate * (1.0 + gate_sum * (1.0 - sigmoid_gate))
    d_up = back_sum * gate_sum * sigmoid_gate
    return hidden.astype(BF), jnp.stack([d_gate.astype(BF), d_up.astype(BF)])


def pipeline(cap, place, rank, x0, g0, received0, mine_x, other_x, mine_g, other_g, w_gate, w_up, w_down, sums):
    r0, r1 = x0.shape[0] // 8, cap // 16
    weights = (w_gate, w_up, w_down)
    units = w_gate.shape[0]
    block = (rank % (8 * r1)) // r1
    dxl, dy = (block + place[1]) % 2, (block // 2 + 4 - place[0]) % 4
    at = jnp.where(rank >= 8 * r1, dy * 2 + dxl + 8, dxl * 4 + dy) * r1 + rank % r1
    rank = jnp.where(rank < 0, -1, at)

    def near_far(total, rows):
        return total[:, :rows], shift(total[:, rows:].astype(BF), "xl", 2, 1).astype(F32)

    total0 = add(received0)
    received0 = over_y([total0[:, :r0]] + [total0[:, k * r0 : (k + 1) * r0].astype(BF) for k in (1, 2, 3)], 1)
    (rank,) = after(received0[1], rank)
    halves = (mine_x, other_x, mine_g, other_g)
    xa, ga, near_a, far_a = project(place, (rank[None, :], *halves), weights, r1, False)
    far_a = shift(far_a, "xl", 2, 1)
    h0, s0 = swiglu_back(add(after(xa, *received0)))
    all0 = over_y([s0] * 4, -1)
    (rank_b,) = after(s0, rank)
    xb, gb, *parts_b = project(place, (rank_b[None, :] - 8 * r1, *halves), weights, r1, True)
    received_b = over_y(parts_b, 1)
    all0 = pack_rows(place, after(xb, *all0))
    pieces0 = [all0, shift(all0, "xl", 2, 1)]
    total_a = add(after(all0, near_a, far_a))
    received_a = over_y([total_a[:, :r1]] + [total_a[:, k * r1 : (k + 1) * r1].astype(BF) for k in (1, 2, 3)], 1)
    near_b, far_b = near_far(add(after(received_a[0], *received_b)), r1)
    ha, sa = swiglu_back(add(after(near_b, *received_a)))
    all_a = over_y([sa] * 4, -1)
    near_b, far_b = after(sa, near_b, far_b)
    hb, sb = swiglu_back(near_b + far_b)
    swap_b = shift(sb, "xl", 2, 1)
    h_all = jnp.concatenate([h0, ha, hb], axis=0)[None]
    swap_h = shift(h_all, "xl", 2, 1)
    pair_h = pack_rows(place, after(sb, h_all, swap_h))
    all_a = pack_rows(place, after(pair_h, *all_a))
    pieces_a = [all_a, shift(all_a, "xl", 2, 1)]
    pair_b = pack_rows(place, after(all_a, sb, swap_b))
    all_b = over_y([pair_b] * 4, -1)
    all_h = over_y([pair_h] * 4, -1)

    def jobs0(y, xl):
        return [
            (i, span((((y + k) % 4) * 2 + (xl + d) % 2) * r0, r0), d, (i, span(k * r0, r0)))
            for d in (0, 1) for k in range(4) for i in (0, 1)
        ]

    def jobs1(y, xl):
        jobs = [(i, span(n * 4 * r1, 4 * r1), n, (i, span(0, 4 * r1))) for n in range(2) for i in (0, 1)]
        return jobs + [(i, span((8 + 2 * n) * r1, 2 * r1), 2 + n, (i, span(0, 2 * r1))) for n in range(4) for i in (0, 1)]

    dgd, dud, *halves = unproject(place, after(pair_b, pieces0[1], *pieces_a, *all_b)[1:], jobs1, cap, weights[:2], rank[:, None])
    swap1 = shift(halves[1], "c", 2, 1)
    dg0, du0, *halves0 = unproject(place, after(dgd, *pieces0), jobs0, 8 * r0, weights[:2], None)
    swap0 = shift(halves0[1], "c", 2, 1)
    xd, gd = jnp.concatenate([xa, xb], axis=0), jnp.concatenate([ga, gb], axis=0)

    def outer(total, first, late, other_first, other_late):
        return (total + dot(first[:, :units], other_first, (0, 0)) + dot(late[:, :units], other_late, (0, 0))).astype(BF)

    rows0, rows1, width = r0 // 2, halves[0].shape[0] // 8, x0.shape[1]
    own1, swap1 = after(dg0, halves[0], swap1)
    total1 = (own1.astype(F32) + swap1.astype(F32)).reshape(2, 4, rows1, width)
    left, right = total1[..., : width // 2], total1[..., width // 2 :]
    far_left = shift(left[1].astype(BF), "xh", 2, 1)
    far_right = [shift(right[:, k].astype(BF), "z", 4, k) for k in (1, 2, 3)]
    (xd_late,) = after(total1, xd)
    grad_gate = outer(sums[2], dg0, dgd, x0, xd_late)
    own0, swap0, far_left, *far_right = after(grad_gate, halves0[0], swap0, far_left, *far_right)
    total0 = own0.astype(F32) + swap0.astype(F32)
    far0 = shift(total0[4 * rows0 :].astype(BF), "xh", 2, 1)
    left = left[0] + far_left.astype(F32)
    right = right[:, 0] + sum(f.astype(F32) for f in far_right)
    far_left = [shift(left[k].astype(BF), "z", 4, k) for k in (1, 2, 3)]
    far_right = shift(right[1].astype(BF), "xh", 2, 1)
    (xd_late,) = after((left[0] + right[0]).astype(BF), xd_late)
    grad_up = outer(sums[3], du0, dud, x0, xd_late)
    far0, far_right, *far_left = after(grad_up, far0, far_right, *far_left)
    total0 = total0[: 4 * rows0] + far0.astype(F32)
    out0 = total0[:rows0] + sum(shift(total0[k * rows0 : (k + 1) * rows0].astype(BF), "z", 4, k).astype(F32) for k in (1, 2, 3))
    out1 = jnp.concatenate([left[0] + sum(f.astype(F32) for f in far_left), right[0] + far_right.astype(F32)], axis=1)
    pieces = after(grad_up, *all_h)
    total = r0 + 2 * r1

    def copies(y, xl):
        jobs = []
        for k in range(4):
            for d in (0, 1):
                here = ((y + k) % 4) * 2 + (xl + d) % 2
                low = d * total
                jobs.append((0, span(here * r0, r0), k, (0, span(low, r0))))
                jobs.append((1, span((4 * d + k) * r1, r1), k, (0, span(low + r0, r1))))
                jobs.append((1, span((8 + 2 * k + d) * r1, r1), k, (0, span(low + r0 + r1, r1))))
        return jobs

    hidden0, hidden_d = move(place, pieces, [(8 * r0, h0.shape[1]), (cap, h0.shape[1])], copies)
    grad_down = outer(sums[4], hidden0, hidden_d, g0, gd)
    return (sums[0] + out0).astype(BF), (sums[1] + out1).astype(BF), grad_gate, grad_up, grad_down


def shards(activations, output_grad, tile_counts, w_gate, w_up, w_down):
    own_rows, width = activations.shape
    tiles, n_tiles = own_rows // TILE, tile_counts.shape[0]
    tail = TILE - HEAD
    y, xl = lax.axis_index("y"), lax.axis_index("xl")
    xh, z, c = lax.axis_index("xh"), lax.axis_index("z"), lax.axis_index("c")
    place = jnp.stack([y, xl]).astype(jnp.int32)
    live = jnp.sum(tile_counts) - HEAD * n_tiles

    w_gate, w_up = w_gate.T, w_up.T

    def one_pass(state):
        step, sums = state
        sums = [jnp.where(step > 0, value.astype(F32), 0.0) for value in sums]
        acts = activations.reshape(tiles, TILE, width)
        grads = output_grad.reshape(tiles, TILE, width)
        first = (step == 0).astype(BF) * jnp.concatenate([acts[:, :HEAD].reshape(-1, width), grads[:, :HEAD].reshape(-1, width)], axis=0)
        rows = tiles * HEAD
        far = shift(first, "xh", 2, 1)
        pair = join(place, [first, far])
        late_x, late_g = acts[:, HEAD:].reshape(-1, width), grads[:, HEAD:].reshape(-1, width)
        late_x, late_g = after(pair, late_x, late_g)
        moved_x = over_z(late_x)
        far_g = shift(late_g, "xh", 2, 1)
        mine = by_core(place, over_z(pair), 2 * rows)
        other = shift(mine, "c", 2, 1)
        pair_g = join(place, after(mine, late_g, far_g))
        moved_g = over_z(pair_g)
        mine, other = after(pair_g, mine, other)
        x0, g0 = move(
            place, [mine, other], [(16 * rows, width)] * 2,
            lambda y, xl: [(i, span((8 * d + n) * rows, rows), d, span((2 * n + i) * rows, rows)) for d in (0, 1) for n in range(8) for i in (0, 1)],
        )
        near_x = join(place, after(x0, *moved_x))
        far_x = shift(near_x, "xh", 2, 1)
        parts0 = project(place, after(near_x, x0, g0), (w_gate, w_up, w_down), x0.shape[0] // 8, False)
        received0 = (parts0[0], shift(parts0[1], "xl", 2, 1))
        mine_g = by_core(place, after(parts0[0], *moved_g), late_x.shape[0])
        mine_x = join(place, after(mine_g, near_x, far_x))
        halves = (mine_x, shift(mine_x, "c", 2, 1), mine_g, shift(mine_g, "c", 2, 1))
        order = lax.iota(jnp.int32, n_tiles)
        dev, sub = order // tiles, order % tiles
        source = (((xh + (dev // 4) % 2) % 2) * 4 + (z + dev % 4) % 4) * 2 + (c + dev // 8) % 2
        wanted = source * tiles + sub
        counts = jnp.sum(jnp.where(wanted[:, None] == order[None, :], tile_counts[None, :], 0), axis=1)
        extra = counts - HEAD
        before = jnp.sum(jnp.where(order[None, :] < order[:, None], extra[None, :], 0), axis=1)
        slot = lax.iota(jnp.int32, tail)
        rank = jnp.where(slot[None, :] < extra[:, None], before[:, None] + slot[None, :], -1).reshape(-1)
        here = rank - step * CAP
        here = jnp.where((rank >= 0) & (here >= 0) & (here < CAP), here, -1)
        results = pipeline(CAP, place, here, x0, g0, received0, *halves, w_gate, w_up, w_down, sums)
        return step + 1, results

    rows = tiles * HEAD
    shapes = ((rows, width), (own_rows - rows, width), w_gate.shape, w_up.shape, w_down.shape)
    start = (jnp.int32(0), tuple(blank(shapes)))
    _, sums = lax.while_loop(lambda state: state[0] * CAP < jnp.maximum(live, 1), one_pass, start)
    out0, out1, grad_gate, grad_up, grad_down = sums
    input_grad = jnp.concatenate([out0.reshape(tiles, HEAD, width), out1.reshape(tiles, tail, width)], axis=1)
    return (input_grad.reshape(own_rows, width), grad_gate.T, grad_up.T, grad_down)


def solution(mesh):
    fine = Mesh(mesh.devices.reshape(4, 2, 2, 4, 2), ("y", "xl", "xh", "z", "c"))
    row, col = ("y", "xl"), ("xh", "z", "c")
    in_specs = (P(col, row), P(col, row), P(), P(row, col), P(row, col), P(col, row))
    out_specs = (P(col, row), P(row, col), P(row, col), P(col, row))
    return jax.shard_map(shards, mesh=fine, in_specs=in_specs, out_specs=out_specs, check_vma=False)
```

```python
import jax
import jax.numpy as jnp
from jax import lax
from jax.experimental import pallas as pl
from jax.experimental.pallas import tpu as pltpu
from jax.sharding import Mesh, PartitionSpec as P

TILE = 64
HEAD = 16
CAP = 1024
BF = jnp.bfloat16
F32 = jnp.float32


def dot(left, right, dims):
    return lax.dot_general(left, right, ((dims[:1], dims[1:]), ((), ())), preferred_element_type=F32)


def shift(value, axis, size, step):
    return lax.ppermute(value, axis, [(i, (i + step) % size) for i in range(size)])


def move(place, sources, shapes, copies):
    count = len(copies(0, 0))

    def kernel(place_ref, *refs):
        ins, outs, sems = refs[: len(sources)], refs[len(sources) : -1], refs[-1]
        jobs = [
            pltpu.make_async_copy(ins[i].at[src], outs[o].at[dst], sems.at[n])
            for n, (o, dst, i, src) in enumerate(copies(place_ref[0], place_ref[1]))
        ]
        for job in jobs:
            job.start()
        for job in jobs:
            job.wait()

    anywhere = pl.BlockSpec(memory_space=pl.ANY)
    return pl.pallas_call(
        kernel,
        out_shape=[jax.ShapeDtypeStruct(s, BF) for s in shapes],
        in_specs=[pl.BlockSpec(memory_space=pltpu.SMEM)] + [anywhere] * len(sources),
        out_specs=[pl.BlockSpec(memory_space=pltpu.VMEM)] * len(shapes),
        scratch_shapes=[pltpu.SemaphoreType.DMA((count,))],
    )(place, *sources)


def after(token, *values):
    return lax.optimization_barrier((*values, token))[:-1]


def blank(shapes):
    return pl.pallas_call(
        lambda *refs: None,
        out_shape=[jax.ShapeDtypeStruct(s, BF) for s in shapes],
        out_specs=[pl.BlockSpec(memory_space=pl.ANY)] * len(shapes),
    )()


def span(start, size):
    return pl.ds(start if isinstance(start, int) else pl.multiple_of(start, 8), size)


def join(place, blocks):
    rows, width = blocks[0].shape
    return move(place, blocks, [(len(blocks) * rows, width)], lambda y, xl: [(0, span(n * rows, rows), n, span(0, rows)) for n in range(len(blocks))])[0]


def by_core(place, moved, rows):
    return move(
        place, moved, [(8 * rows, moved[0].shape[1])],
        lambda y, xl: [(0, span((4 * d + n) * rows, rows), n, span(d * rows, rows)) for n in range(4) for d in (0, 1)],
    )[0]


def over_z(value):
    return [value] + [shift(value, "z", 4, -k) for k in (1, 2, 3)]


def project(place, sources, weights, rows, y_first):
    units, width = weights[0].shape
    wide = -(-units // 128) * 128
    compact = len(sources) > 2
    total = 8 * rows
    if y_first:
        cuts = [(k * 2 * rows, 2 * rows) for k in range(4)]
    else:
        cuts = [(n * 4 * rows, 4 * rows) for n in range(2)]
    shapes = [(3, size, wide) for _, size in cuts]
    if compact:
        shapes = [(total, width)] * 2 + shapes
    n_in = len(sources) + 3

    def kernel(place_ref, *refs):
        ins, w_refs, outs = refs[: len(sources)], refs[len(sources) : n_in], refs[n_in : n_in + len(shapes)]
        bufs, sems = refs[n_in + len(shapes) : -1], refs[-1]
        jobs = []

        def start(src, dst):
            job = pltpu.make_async_copy(src, dst, sems.at[len(jobs)])
            job.start()
            jobs.append(job)
            return job

        if compact:
            rank = ins[0][...]
            feeds = [start(ins[1 + i], bufs[3 + i]) for i in range(4)]
        else:
            feeds = []
            for i in (0, 1):
                for k in range(4):
                    for d in (0, 1):
                        block = ((place_ref[0] + k) % 4) * 2 + (place_ref[1] + d) % 2
                        feeds.append(start(ins[i].at[span(block * rows, rows)], bufs[3 + i].at[span((2 * k + d) * rows, rows)]))
        loads = [start(w_refs[i], bufs[i]) for i in range(3)]
        if compact:
            pick = (lax.broadcasted_iota(jnp.int32, (total, rank.shape[1]), 0) == rank).astype(F32).astype(BF)
            half = rank.shape[1] // 2
            for i in (0, 1):
                feeds[2 * i].wait()
                feeds[2 * i + 1].wait()
                outs[i][...] = (dot(pick[:, :half], bufs[3 + 2 * i][...], (1, 0)) + dot(pick[:, half:], bufs[4 + 2 * i][...], (1, 0))).astype(BF)
            lefts = outs[:2]
            packs = outs[2:]
        else:
            for feed in feeds:
                feed.wait()
            lefts = bufs[3:5]
            packs = outs
        for i in range(3):
            loads[i].wait()
            for (low, size), out in zip(cuts, packs):
                left = lefts[i // 2][low : low + size]
                out[i, :, :units] = dot(left, bufs[i][...], (1, 1)).astype(BF)
                out[i, :, units:] = jnp.zeros((size, wide - units), BF)

    anywhere = pl.BlockSpec(memory_space=pl.ANY)
    vmem = pl.BlockSpec(memory_space=pltpu.VMEM)
    smem = pl.BlockSpec(memory_space=pltpu.SMEM)
    scratch = [pltpu.VMEM(w.shape, BF) for w in weights]
    scratch += [pltpu.VMEM(s.shape, BF) for s in (sources[1:] if compact else sources)]
    return pl.pallas_call(
        kernel,
        out_shape=[jax.ShapeDtypeStruct(s, BF) for s in shapes],
        in_specs=[smem] + ([vmem] if compact else []) + [anywhere] * (n_in - compact),
        out_specs=[vmem] * len(shapes),
        scratch_shapes=scratch + [pltpu.SemaphoreType.DMA((19,))],
    )(place, *sources, *weights)


def unproject(place, pieces, jobs_of, total, weights, rank_col):
    units, width = weights[0].shape
    wide = pieces[0].shape[-1]
    arrays = list(pieces)
    expand = rank_col is not None
    half = (rank_col.shape[0] if expand else total) // 2
    count = len(jobs_of(0, 0))

    def kernel(place_ref, *refs):
        ins, w_refs = refs[: len(arrays)], refs[len(arrays) : len(arrays) + 2]
        rest = refs[len(arrays) + 2 :]
        if expand:
            rank, rest = rest[0][...], rest[1:]
        outs, bufs, sems = rest[:4], rest[4:6], rest[6]
        jobs = [
            pltpu.make_async_copy(ins[i].at[src], outs[o].at[dst], sems.at[n])
            for n, (o, dst, i, src) in enumerate(jobs_of(place_ref[0], place_ref[1]))
        ]
        jobs += [pltpu.make_async_copy(w_refs[i], bufs[i], sems.at[count + i]) for i in (0, 1)]
        for job in jobs:
            job.start()
        for job in jobs:
            job.wait()
        if expand:
            part = (dot(outs[0][:, :units], bufs[0][...], (1, 0)) + dot(outs[1][:, :units], bufs[1][...], (1, 0))).astype(BF)
            pick = (rank == lax.broadcasted_iota(jnp.int32, (rank.shape[0], total), 1)).astype(F32).astype(BF)
            for n in (0, 1):
                outs[2 + n][...] = dot(pick[n * half : (n + 1) * half], part, (1, 0)).astype(BF)
        else:
            for n in (0, 1):
                rows = slice(n * half, (n + 1) * half)
                outs[2 + n][...] = (dot(outs[0][rows, :units], bufs[0][...], (1, 0)) + dot(outs[1][rows, :units], bufs[1][...], (1, 0))).astype(BF)

    anywhere = pl.BlockSpec(memory_space=pl.ANY)
    vmem = pl.BlockSpec(memory_space=pltpu.VMEM)
    shapes = [(total, wide)] * 2 + [(half, width)] * 2
    return pl.pallas_call(
        kernel,
        out_shape=[jax.ShapeDtypeStruct(s, BF) for s in shapes],
        in_specs=[pl.BlockSpec(memory_space=pltpu.SMEM)] + [anywhere] * (len(arrays) + 2) + [vmem] * expand,
        out_specs=[vmem] * 4,
        scratch_shapes=[pltpu.VMEM((units, width), BF)] * 2 + [pltpu.SemaphoreType.DMA((count + 2,))],
    )(place, *arrays, *weights, *([rank_col] if expand else []))


def over_y(blocks, step):
    return [blocks[0]] + [shift(blocks[k], "y", 4, step * k) for k in (1, 2, 3)]


def add(blocks):
    return sum(b.astype(F32) for b in blocks[1:]) + blocks[0].astype(F32)


def pack_rows(place, blocks):
    n, rows, width = blocks[0].shape
    return move(
        place, blocks, [(n, len(blocks) * rows, width)],
        lambda y, xl: [(0, (i, span(k * rows, rows)), k, (i, span(0, rows))) for k in range(len(blocks)) for i in range(n)],
    )[0]


def swiglu_back(totals):
    gate_sum, up_sum, back_sum = totals[0], totals[1], totals[2]
    sigmoid_gate = jax.nn.sigmoid(gate_sum)
    hidden = gate_sum * sigmoid_gate * up_sum
    d_gate = back_sum * up_sum * sigmoid_gate * (1.0 + gate_sum * (1.0 - sigmoid_gate))
    d_up = back_sum * gate_sum * sigmoid_gate
    return hidden.astype(BF), jnp.stack([d_gate.astype(BF), d_up.astype(BF)])


def pipeline(cap, place, rank, x0, g0, received0, mine_x, other_x, mine_g, other_g, w_gate, w_up, w_down, sums):
    r0, r1 = x0.shape[0] // 8, cap // 16
    weights = (w_gate, w_up, w_down)
    units = w_gate.shape[0]
    block = (rank % (8 * r1)) // r1
    dxl, dy = (block + place[1]) % 2, (block // 2 + 4 - place[0]) % 4
    at = jnp.where(rank >= 8 * r1, dy * 2 + dxl + 8, dxl * 4 + dy) * r1 + rank % r1
    rank = jnp.where(rank < 0, -1, at)

    def near_far(total, rows):
        return total[:, :rows], shift(total[:, rows:].astype(BF), "xl", 2, 1).astype(F32)

    halves = (mine_x, other_x, mine_g, other_g)
    xa, ga, near_a, far_a = project(place, (rank[None, :], *halves), weights, r1, False)
    far_a = shift(far_a, "xl", 2, 1)
    near0, far0 = near_far(add(after(xa, *received0)), r0)
    (rank_b,) = after(near0, rank)
    xb, gb, *parts_b = project(place, (rank_b[None, :] - 8 * r1, *halves), weights, r1, True)
    received_b = over_y(parts_b, 1)
    total_a = add(after(xb, near_a, far_a))
    received_a = over_y([total_a[:, :r1]] + [total_a[:, k * r1 : (k + 1) * r1].astype(BF) for k in (1, 2, 3)], 1)
    near_b, far_b = near_far(add(after(received_a[0], *received_b)), r1)
    near0, far0 = after(near_b, near0, far0)
    h0, s0 = swiglu_back(near0 + far0)
    swap_s0 = shift(s0, "xl", 2, 1)
    ha, sa = swiglu_back(add(after(s0, *received_a)))
    all_a = over_y([sa] * 4, -1)
    pair0 = pack_rows(place, after(sa, s0, swap_s0))
    near_b, far_b = after(pair0, near_b, far_b)
    hb, sb = swiglu_back(near_b + far_b)
    swap_b = shift(sb, "xl", 2, 1)
    h_all = jnp.concatenate([h0, ha, hb], axis=0)[None]
    swap_h = shift(h_all, "xl", 2, 1)
    pair_h = pack_rows(place, after(sb, h_all, swap_h))
    all_a = pack_rows(place, after(pair_h, *all_a))
    pieces_a = [all_a, shift(all_a, "xl", 2, 1)]
    pair_b = pack_rows(place, after(all_a, sb, swap_b))
    all_b = over_y([pair_b] * 4, -1)
    pieces0 = over_y([pair0] * 4, -1)
    all_h = over_y([pair_h] * 4, -1)

    def jobs0(y, xl):
        return [
            (i, span((((y + k) % 4) * 2 + (xl + d) % 2) * r0, r0), k, (i, span(d * r0, r0)))
            for d in (0, 1) for k in range(4) for i in (0, 1)
        ]

    def jobs1(y, xl):
        jobs = [(i, span(n * 4 * r1, 4 * r1), n, (i, span(0, 4 * r1))) for n in range(2) for i in (0, 1)]
        return jobs + [(i, span((8 + 2 * n) * r1, 2 * r1), 2 + n, (i, span(0, 2 * r1))) for n in range(4) for i in (0, 1)]

    dgd, dud, *halves = unproject(place, after(pair_b, *pieces0[1:], *pieces_a, *all_b)[3:], jobs1, cap, weights[:2], rank[:, None])
    swap1 = shift(halves[1], "c", 2, 1)
    dg0, du0, *halves0 = unproject(place, after(dgd, *pieces0), jobs0, 8 * r0, weights[:2], None)
    swap0 = shift(halves0[1], "c", 2, 1)
    xd, gd = jnp.concatenate([xa, xb], axis=0), jnp.concatenate([ga, gb], axis=0)

    def outer(total, first, late, other_first, other_late):
        return (total + dot(first[:, :units], other_first, (0, 0)) + dot(late[:, :units], other_late, (0, 0))).astype(BF)

    rows0, rows1, width = r0 // 2, halves[0].shape[0] // 8, x0.shape[1]
    own1, swap1 = after(dgd, halves[0], swap1)
    total1 = (own1.astype(F32) + swap1.astype(F32)).reshape(2, 4, rows1, width)
    left, right = total1[..., : width // 2], total1[..., width // 2 :]
    far_left = shift(left[1].astype(BF), "xh", 2, 1)
    far_right = [shift(right[:, k].astype(BF), "z", 4, k) for k in (1, 2, 3)]
    (xd_late,) = after(total1, xd)
    grad_gate = outer(sums[2], dg0, dgd, x0, xd_late)
    own0, swap0, far_left, *far_right = after(grad_gate, halves0[0], swap0, far_left, *far_right)
    total0 = own0.astype(F32) + swap0.astype(F32)
    far0 = shift(total0[4 * rows0 :].astype(BF), "xh", 2, 1)
    left = left[0] + far_left.astype(F32)
    right = right[:, 0] + sum(f.astype(F32) for f in far_right)
    far_left = [shift(left[k].astype(BF), "z", 4, k) for k in (1, 2, 3)]
    far_right = shift(right[1].astype(BF), "xh", 2, 1)
    (xd_late,) = after((left[0] + right[0]).astype(BF), xd_late)
    grad_up = outer(sums[3], du0, dud, x0, xd_late)
    far0, far_right, *far_left = after(grad_up, far0, far_right, *far_left)
    total0 = total0[: 4 * rows0] + far0.astype(F32)
    out0 = total0[:rows0] + sum(shift(total0[k * rows0 : (k + 1) * rows0].astype(BF), "z", 4, k).astype(F32) for k in (1, 2, 3))
    out1 = jnp.concatenate([left[0] + sum(f.astype(F32) for f in far_left), right[0] + far_right.astype(F32)], axis=1)
    pieces = after(grad_up, *all_h)
    total = r0 + 2 * r1

    def copies(y, xl):
        jobs = []
        for k in range(4):
            for d in (0, 1):
                here = ((y + k) % 4) * 2 + (xl + d) % 2
                low = d * total
                jobs.append((0, span(here * r0, r0), k, (0, span(low, r0))))
                jobs.append((1, span((4 * d + k) * r1, r1), k, (0, span(low + r0, r1))))
                jobs.append((1, span((8 + 2 * k + d) * r1, r1), k, (0, span(low + r0 + r1, r1))))
        return jobs

    hidden0, hidden_d = move(place, pieces, [(8 * r0, h0.shape[1]), (cap, h0.shape[1])], copies)
    grad_down = outer(sums[4], hidden0, hidden_d, g0, gd)
    return (sums[0] + out0).astype(BF), (sums[1] + out1).astype(BF), grad_gate, grad_up, grad_down


def shards(activations, output_grad, tile_counts, w_gate, w_up, w_down):
    own_rows, width = activations.shape
    tiles, n_tiles = own_rows // TILE, tile_counts.shape[0]
    tail = TILE - HEAD
    y, xl = lax.axis_index("y"), lax.axis_index("xl")
    xh, z, c = lax.axis_index("xh"), lax.axis_index("z"), lax.axis_index("c")
    place = jnp.stack([y, xl]).astype(jnp.int32)
    live = jnp.sum(tile_counts) - HEAD * n_tiles

    w_gate, w_up = w_gate.T, w_up.T

    def one_pass(state):
        step, sums = state
        sums = [jnp.where(step > 0, value.astype(F32), 0.0) for value in sums]
        acts = activations.reshape(tiles, TILE, width)
        grads = output_grad.reshape(tiles, TILE, width)
        first = (step == 0).astype(BF) * jnp.concatenate([acts[:, :HEAD].reshape(-1, width), grads[:, :HEAD].reshape(-1, width)], axis=0)
        rows = tiles * HEAD
        far = shift(first, "xh", 2, 1)
        pair = join(place, [first, far])
        late_x, late_g = acts[:, HEAD:].reshape(-1, width), grads[:, HEAD:].reshape(-1, width)
        late_x, late_g = after(pair, late_x, late_g)
        moved_x = over_z(late_x)
        far_g = shift(late_g, "xh", 2, 1)
        mine = by_core(place, over_z(pair), 2 * rows)
        other = shift(mine, "c", 2, 1)
        pair_g = join(place, after(mine, late_g, far_g))
        moved_g = over_z(pair_g)
        mine, other = after(pair_g, mine, other)
        x0, g0 = move(
            place, [mine, other], [(16 * rows, width)] * 2,
            lambda y, xl: [(i, span((8 * d + n) * rows, rows), d, span((2 * n + i) * rows, rows)) for d in (0, 1) for n in range(8) for i in (0, 1)],
        )
        near_x = join(place, after(x0, *moved_x))
        far_x = shift(near_x, "xh", 2, 1)
        parts0 = project(place, after(near_x, x0, g0), (w_gate, w_up, w_down), x0.shape[0] // 8, True)
        received0 = over_y(parts0, 1)
        mine_g = by_core(place, after(parts0[0], received0[1], received0[3], *moved_g)[2:], late_x.shape[0])
        mine_x = join(place, after(mine_g, near_x, far_x))
        halves = (mine_x, shift(mine_x, "c", 2, 1), mine_g, shift(mine_g, "c", 2, 1))
        order = lax.iota(jnp.int32, n_tiles)
        dev, sub = order // tiles, order % tiles
        source = (((xh + (dev // 4) % 2) % 2) * 4 + (z + dev % 4) % 4) * 2 + (c + dev // 8) % 2
        wanted = source * tiles + sub
        counts = jnp.sum(jnp.where(wanted[:, None] == order[None, :], tile_counts[None, :], 0), axis=1)
        extra = counts - HEAD
        before = jnp.sum(jnp.where(order[None, :] < order[:, None], extra[None, :], 0), axis=1)
        slot = lax.iota(jnp.int32, tail)
        rank = jnp.where(slot[None, :] < extra[:, None], before[:, None] + slot[None, :], -1).reshape(-1)
        here = rank - step * CAP
        here = jnp.where((rank >= 0) & (here >= 0) & (here < CAP), here, -1)
        results = pipeline(CAP, place, here, x0, g0, received0, *halves, w_gate, w_up, w_down, sums)
        return step + 1, results

    rows = tiles * HEAD
    shapes = ((rows, width), (own_rows - rows, width), w_gate.shape, w_up.shape, w_down.shape)
    start = (jnp.int32(0), tuple(blank(shapes)))
    _, sums = lax.while_loop(lambda state: state[0] * CAP < jnp.maximum(live, 1), one_pass, start)
    out0, out1, grad_gate, grad_up, grad_down = sums
    input_grad = jnp.concatenate([out0.reshape(tiles, HEAD, width), out1.reshape(tiles, tail, width)], axis=1)
    return (input_grad.reshape(own_rows, width), grad_gate.T, grad_up.T, grad_down)


def solution(mesh):
    fine = Mesh(mesh.devices.reshape(4, 2, 2, 4, 2), ("y", "xl", "xh", "z", "c"))
    row, col = ("y", "xl"), ("xh", "z", "c")
    in_specs = (P(col, row), P(col, row), P(), P(row, col), P(row, col), P(col, row))
    out_specs = (P(col, row), P(row, col), P(row, col), P(col, row))
    return jax.shard_map(shards, mesh=fine, in_specs=in_specs, out_specs=out_specs, check_vma=False)
```

```python
import jax
import jax.numpy as jnp
from jax import lax
from jax.experimental import pallas as pl
from jax.experimental.pallas import tpu as pltpu
from jax.sharding import Mesh, PartitionSpec as P

TILE = 64
HEAD = 16
CAP = 1024
BF = jnp.bfloat16
F32 = jnp.float32


def dot(left, right, dims):
    return lax.dot_general(left, right, ((dims[:1], dims[1:]), ((), ())), preferred_element_type=F32)


def shift(value, axis, size, step):
    return lax.ppermute(value, axis, [(i, (i + step) % size) for i in range(size)])


def move(place, sources, shapes, copies):
    count = len(copies(0, 0))

    def kernel(place_ref, *refs):
        ins, outs, sems = refs[: len(sources)], refs[len(sources) : -1], refs[-1]
        jobs = [
            pltpu.make_async_copy(ins[i].at[src], outs[o].at[dst], sems.at[n])
            for n, (o, dst, i, src) in enumerate(copies(place_ref[0], place_ref[1]))
        ]
        for job in jobs:
            job.start()
        for job in jobs:
            job.wait()

    anywhere = pl.BlockSpec(memory_space=pl.ANY)
    return pl.pallas_call(
        kernel,
        out_shape=[jax.ShapeDtypeStruct(s, BF) for s in shapes],
        in_specs=[pl.BlockSpec(memory_space=pltpu.SMEM)] + [anywhere] * len(sources),
        out_specs=[pl.BlockSpec(memory_space=pltpu.VMEM)] * len(shapes),
        scratch_shapes=[pltpu.SemaphoreType.DMA((count,))],
    )(place, *sources)


def after(token, *values):
    return lax.optimization_barrier((*values, token))[:-1]


def blank(shapes):
    return pl.pallas_call(
        lambda *refs: None,
        out_shape=[jax.ShapeDtypeStruct(s, BF) for s in shapes],
        out_specs=[pl.BlockSpec(memory_space=pl.ANY)] * len(shapes),
    )()


def span(start, size):
    return pl.ds(start if isinstance(start, int) else pl.multiple_of(start, 8), size)


def join(place, blocks):
    rows, width = blocks[0].shape
    return move(place, blocks, [(len(blocks) * rows, width)], lambda y, xl: [(0, span(n * rows, rows), n, span(0, rows)) for n in range(len(blocks))])[0]


def by_core(place, moved, rows):
    return move(
        place, moved, [(8 * rows, moved[0].shape[1])],
        lambda y, xl: [(0, span((4 * d + n) * rows, rows), n, span(d * rows, rows)) for n in range(4) for d in (0, 1)],
    )[0]


def over_z(value):
    return [value] + [shift(value, "z", 4, -k) for k in (1, 2, 3)]


def project(place, sources, weights, rows, y_first):
    units, width = weights[0].shape
    wide = -(-units // 128) * 128
    compact = len(sources) > 2
    total = 8 * rows
    if y_first:
        cuts = [(k * 2 * rows, 2 * rows) for k in range(4)]
    else:
        cuts = [(n * 4 * rows, 4 * rows) for n in range(2)]
    shapes = [(3, size, wide) for _, size in cuts]
    if compact:
        shapes = [(total, width)] * 2 + shapes
    n_in = len(sources) + 3

    def kernel(place_ref, *refs):
        ins, w_refs, outs = refs[: len(sources)], refs[len(sources) : n_in], refs[n_in : n_in + len(shapes)]
        bufs, sems = refs[n_in + len(shapes) : -1], refs[-1]
        jobs = []

        def start(src, dst):
            job = pltpu.make_async_copy(src, dst, sems.at[len(jobs)])
            job.start()
            jobs.append(job)
            return job

        if compact:
            rank = ins[0][...]
            feeds = [start(ins[1 + i], bufs[3 + i]) for i in range(4)]
        else:
            feeds = []
            for i in (0, 1):
                for k in range(4):
                    for d in (0, 1):
                        block = ((place_ref[0] + k) % 4) * 2 + (place_ref[1] + d) % 2
                        feeds.append(start(ins[i].at[span(block * rows, rows)], bufs[3 + i].at[span((2 * k + d) * rows, rows)]))
        loads = [start(w_refs[i], bufs[i]) for i in range(3)]
        if compact:
            pick = (lax.broadcasted_iota(jnp.int32, (total, rank.shape[1]), 0) == rank).astype(F32).astype(BF)
            half = rank.shape[1] // 2
            for i in (0, 1):
                feeds[2 * i].wait()
                feeds[2 * i + 1].wait()
                outs[i][...] = (dot(pick[:, :half], bufs[3 + 2 * i][...], (1, 0)) + dot(pick[:, half:], bufs[4 + 2 * i][...], (1, 0))).astype(BF)
            lefts = outs[:2]
            packs = outs[2:]
        else:
            for feed in feeds:
                feed.wait()
            lefts = bufs[3:5]
            packs = outs
        for i in range(3):
            loads[i].wait()
            for (low, size), out in zip(cuts, packs):
                left = lefts[i // 2][low : low + size]
                out[i, :, :units] = dot(left, bufs[i][...], (1, 1)).astype(BF)
                out[i, :, units:] = jnp.zeros((size, wide - units), BF)

    anywhere = pl.BlockSpec(memory_space=pl.ANY)
    vmem = pl.BlockSpec(memory_space=pltpu.VMEM)
    smem = pl.BlockSpec(memory_space=pltpu.SMEM)
    scratch = [pltpu.VMEM(w.shape, BF) for w in weights]
    scratch += [pltpu.VMEM(s.shape, BF) for s in (sources[1:] if compact else sources)]
    return pl.pallas_call(
        kernel,
        out_shape=[jax.ShapeDtypeStruct(s, BF) for s in shapes],
        in_specs=[smem] + ([vmem] if compact else []) + [anywhere] * (n_in - compact),
        out_specs=[vmem] * len(shapes),
        scratch_shapes=scratch + [pltpu.SemaphoreType.DMA((19,))],
    )(place, *sources, *weights)


def unproject(place, pieces, jobs_of, total, weights, rank_col):
    units, width = weights[0].shape
    wide = pieces[0].shape[-1]
    arrays = list(pieces)
    expand = rank_col is not None
    half = (rank_col.shape[0] if expand else total) // 2
    count = len(jobs_of(0, 0))

    def kernel(place_ref, *refs):
        ins, w_refs = refs[: len(arrays)], refs[len(arrays) : len(arrays) + 2]
        rest = refs[len(arrays) + 2 :]
        if expand:
            rank, rest = rest[0][...], rest[1:]
        outs, bufs, sems = rest[:4], rest[4:6], rest[6]
        jobs = [
            pltpu.make_async_copy(ins[i].at[src], outs[o].at[dst], sems.at[n])
            for n, (o, dst, i, src) in enumerate(jobs_of(place_ref[0], place_ref[1]))
        ]
        jobs += [pltpu.make_async_copy(w_refs[i], bufs[i], sems.at[count + i]) for i in (0, 1)]
        for job in jobs:
            job.start()
        for job in jobs:
            job.wait()
        if expand:
            part = (dot(outs[0][:, :units], bufs[0][...], (1, 0)) + dot(outs[1][:, :units], bufs[1][...], (1, 0))).astype(BF)
            pick = (rank == lax.broadcasted_iota(jnp.int32, (rank.shape[0], total), 1)).astype(F32).astype(BF)
            for n in (0, 1):
                outs[2 + n][...] = dot(pick[n * half : (n + 1) * half], part, (1, 0)).astype(BF)
        else:
            for n in (0, 1):
                rows = slice(n * half, (n + 1) * half)
                outs[2 + n][...] = (dot(outs[0][rows, :units], bufs[0][...], (1, 0)) + dot(outs[1][rows, :units], bufs[1][...], (1, 0))).astype(BF)

    anywhere = pl.BlockSpec(memory_space=pl.ANY)
    vmem = pl.BlockSpec(memory_space=pltpu.VMEM)
    shapes = [(total, wide)] * 2 + [(half, width)] * 2
    return pl.pallas_call(
        kernel,
        out_shape=[jax.ShapeDtypeStruct(s, BF) for s in shapes],
        in_specs=[pl.BlockSpec(memory_space=pltpu.SMEM)] + [anywhere] * (len(arrays) + 2) + [vmem] * expand,
        out_specs=[vmem] * 4,
        scratch_shapes=[pltpu.VMEM((units, width), BF)] * 2 + [pltpu.SemaphoreType.DMA((count + 2,))],
    )(place, *arrays, *weights, *([rank_col] if expand else []))


def over_y(blocks, step):
    return [blocks[0]] + [shift(blocks[k], "y", 4, step * k) for k in (1, 2, 3)]


def add(blocks):
    return sum(b.astype(F32) for b in blocks[1:]) + blocks[0].astype(F32)


def pack_rows(place, blocks):
    n, rows, width = blocks[0].shape
    return move(
        place, blocks, [(n, len(blocks) * rows, width)],
        lambda y, xl: [(0, (i, span(k * rows, rows)), k, (i, span(0, rows))) for k in range(len(blocks)) for i in range(n)],
    )[0]


def swiglu_back(totals):
    gate_sum, up_sum, back_sum = totals[0], totals[1], totals[2]
    sigmoid_gate = jax.nn.sigmoid(gate_sum)
    hidden = gate_sum * sigmoid_gate * up_sum
    d_gate = back_sum * up_sum * sigmoid_gate * (1.0 + gate_sum * (1.0 - sigmoid_gate))
    d_up = back_sum * gate_sum * sigmoid_gate
    return hidden.astype(BF), jnp.stack([d_gate.astype(BF), d_up.astype(BF)])


def pipeline(cap, place, rank, x0, g0, received0, mine_x, other_x, mine_g, other_g, w_gate, w_up, w_down, sums):
    r0, r1 = x0.shape[0] // 8, cap // 16
    weights = (w_gate, w_up, w_down)
    units = w_gate.shape[0]
    block = (rank % (8 * r1)) // r1
    dxl, dy = (block + place[1]) % 2, (block // 2 + 4 - place[0]) % 4
    at = jnp.where(rank >= 8 * r1, dy * 2 + dxl + 8, dxl * 4 + dy) * r1 + rank % r1
    rank = jnp.where(rank < 0, -1, at)

    def near_far(total, rows):
        return total[:, :rows], shift(total[:, rows:].astype(BF), "xl", 2, 1).astype(F32)

    halves = (mine_x, other_x, mine_g, other_g)
    xa, ga, near_a, far_a = project(place, (rank[None, :], *halves), weights, r1, False)
    far_a = shift(far_a, "xl", 2, 1)
    near0, far0 = near_far(add(after(xa, *received0)), r0)
    (rank_b,) = after(near0, rank)
    xb, gb, *parts_b = project(place, (rank_b[None, :] - 8 * r1, *halves), weights, r1, True)
    received_b = over_y(parts_b, 1)
    total_a = add(after(xb, near_a, far_a))
    received_a = over_y([total_a[:, :r1]] + [total_a[:, k * r1 : (k + 1) * r1].astype(BF) for k in (1, 2, 3)], 1)
    near_b, far_b = near_far(add(after(received_a[0], *received_b)), r1)
    near0, far0 = after(near_b, near0, far0)
    h0, s0 = swiglu_back(near0 + far0)
    swap_s0 = shift(s0, "xl", 2, 1)
    ha, sa = swiglu_back(add(after(s0, *received_a)))
    all_a = over_y([sa] * 4, -1)
    pair0 = pack_rows(place, after(sa, s0, swap_s0))
    near_b, far_b = after(pair0, near_b, far_b)
    hb, sb = swiglu_back(near_b + far_b)
    swap_b = shift(sb, "xl", 2, 1)
    h_all = jnp.concatenate([h0, ha, hb], axis=0)[None]
    swap_h = shift(h_all, "xl", 2, 1)
    pair_h = pack_rows(place, after(sb, h_all, swap_h))
    all_a = pack_rows(place, after(pair_h, *all_a))
    pieces_a = [all_a, shift(all_a, "xl", 2, 1)]
    pair_b = pack_rows(place, after(all_a, sb, swap_b))
    all_b = over_y([pair_b] * 4, -1)
    pieces0 = over_y([pair0] * 4, -1)
    all_h = over_y([pair_h] * 4, -1)

    def jobs0(y, xl):
        return [
            (i, span((((y + k) % 4) * 2 + (xl + d) % 2) * r0, r0), k, (i, span(d * r0, r0)))
            for d in (0, 1) for k in range(4) for i in (0, 1)
        ]

    def jobs1(y, xl):
        jobs = [(i, span(n * 4 * r1, 4 * r1), n, (i, span(0, 4 * r1))) for n in range(2) for i in (0, 1)]
        return jobs + [(i, span((8 + 2 * n) * r1, 2 * r1), 2 + n, (i, span(0, 2 * r1))) for n in range(4) for i in (0, 1)]

    dgd, dud, *halves = unproject(place, after(pair_b, *pieces0[1:], *pieces_a, *all_b)[3:], jobs1, cap, weights[:2], rank[:, None])
    swap1 = shift(halves[1], "c", 2, 1)
    dg0, du0, *halves0 = unproject(place, after(dgd, all_h[1], all_h[3], *pieces0)[2:], jobs0, 8 * r0, weights[:2], None)
    swap0 = shift(halves0[1], "c", 2, 1)
    xd, gd = jnp.concatenate([xa, xb], axis=0), jnp.concatenate([ga, gb], axis=0)

    def outer(total, first, late, other_first, other_late):
        return (total + dot(first[:, :units], other_first, (0, 0)) + dot(late[:, :units], other_late, (0, 0))).astype(BF)

    rows0, rows1, width = r0 // 2, halves[0].shape[0] // 8, x0.shape[1]
    own1, swap1 = after(dg0, halves[0], swap1)
    total1 = (own1.astype(F32) + swap1.astype(F32)).reshape(2, 4, rows1, width)
    left, right = total1[..., : width // 2], total1[..., width // 2 :]
    far_left = shift(left[1].astype(BF), "xh", 2, 1)
    far_right = [shift(right[:, k].astype(BF), "z", 4, k) for k in (1, 2, 3)]
    (xd_late,) = after(total1, xd)
    grad_gate = outer(sums[2], dg0, dgd, x0, xd_late)
    own0, swap0, far_left, *far_right = after(grad_gate, halves0[0], swap0, far_left, *far_right)
    total0 = own0.astype(F32) + swap0.astype(F32)
    far0 = shift(total0[4 * rows0 :].astype(BF), "xh", 2, 1)
    left = left[0] + far_left.astype(F32)
    right = right[:, 0] + sum(f.astype(F32) for f in far_right)
    far_left = [shift(left[k].astype(BF), "z", 4, k) for k in (1, 2, 3)]
    far_right = shift(right[1].astype(BF), "xh", 2, 1)
    (xd_late,) = after((left[0] + right[0]).astype(BF), xd_late)
    grad_up = outer(sums[3], du0, dud, x0, xd_late)
    far0, far_right, *far_left = after(grad_up, far0, far_right, *far_left)
    total0 = total0[: 4 * rows0] + far0.astype(F32)
    out0 = total0[:rows0] + sum(shift(total0[k * rows0 : (k + 1) * rows0].astype(BF), "z", 4, k).astype(F32) for k in (1, 2, 3))
    out1 = jnp.concatenate([left[0] + sum(f.astype(F32) for f in far_left), right[0] + far_right.astype(F32)], axis=1)
    pieces = after(grad_up, *all_h)
    total = r0 + 2 * r1

    def copies(y, xl):
        jobs = []
        for k in range(4):
            for d in (0, 1):
                here = ((y + k) % 4) * 2 + (xl + d) % 2
                low = d * total
                jobs.append((0, span(here * r0, r0), k, (0, span(low, r0))))
                jobs.append((1, span((4 * d + k) * r1, r1), k, (0, span(low + r0, r1))))
                jobs.append((1, span((8 + 2 * k + d) * r1, r1), k, (0, span(low + r0 + r1, r1))))
        return jobs

    hidden0, hidden_d = move(place, pieces, [(8 * r0, h0.shape[1]), (cap, h0.shape[1])], copies)
    grad_down = outer(sums[4], hidden0, hidden_d, g0, gd)
    return (sums[0] + out0).astype(BF), (sums[1] + out1).astype(BF), grad_gate, grad_up, grad_down


def shards(activations, output_grad, tile_counts, w_gate, w_up, w_down):
    own_rows, width = activations.shape
    tiles, n_tiles = own_rows // TILE, tile_counts.shape[0]
    tail = TILE - HEAD
    y, xl = lax.axis_index("y"), lax.axis_index("xl")
    xh, z, c = lax.axis_index("xh"), lax.axis_index("z"), lax.axis_index("c")
    place = jnp.stack([y, xl]).astype(jnp.int32)
    live = jnp.sum(tile_counts) - HEAD * n_tiles

    w_gate, w_up = w_gate.T, w_up.T

    def one_pass(state):
        step, sums = state
        sums = [jnp.where(step > 0, value.astype(F32), 0.0) for value in sums]
        acts = activations.reshape(tiles, TILE, width)
        grads = output_grad.reshape(tiles, TILE, width)
        first = (step == 0).astype(BF) * jnp.concatenate([acts[:, :HEAD].reshape(-1, width), grads[:, :HEAD].reshape(-1, width)], axis=0)
        rows = tiles * HEAD
        far = shift(first, "xh", 2, 1)
        pair = join(place, [first, far])
        late_x, late_g = acts[:, HEAD:].reshape(-1, width), grads[:, HEAD:].reshape(-1, width)
        late_x, late_g = after(pair, late_x, late_g)
        moved_x = over_z(late_x)
        far_g = shift(late_g, "xh", 2, 1)
        mine = by_core(place, over_z(pair), 2 * rows)
        other = shift(mine, "c", 2, 1)
        pair_g = join(place, after(mine, late_g, far_g))
        moved_g = over_z(pair_g)
        mine, other = after(pair_g, mine, other)
        x0, g0 = move(
            place, [mine, other], [(16 * rows, width)] * 2,
            lambda y, xl: [(i, span((8 * d + n) * rows, rows), d, span((2 * n + i) * rows, rows)) for d in (0, 1) for n in range(8) for i in (0, 1)],
        )
        near_x = join(place, after(x0, *moved_x))
        far_x = shift(near_x, "xh", 2, 1)
        parts0 = project(place, after(near_x, x0, g0), (w_gate, w_up, w_down), x0.shape[0] // 8, True)
        received0 = over_y(parts0, 1)
        mine_g = by_core(place, after(parts0[0], received0[1], received0[3], *moved_g)[2:], late_x.shape[0])
        mine_x = join(place, after(mine_g, near_x, far_x))
        halves = (mine_x, shift(mine_x, "c", 2, 1), mine_g, shift(mine_g, "c", 2, 1))
        order = lax.iota(jnp.int32, n_tiles)
        dev, sub = order // tiles, order % tiles
        source = (((xh + (dev // 4) % 2) % 2) * 4 + (z + dev % 4) % 4) * 2 + (c + dev // 8) % 2
        wanted = source * tiles + sub
        counts = jnp.sum(jnp.where(wanted[:, None] == order[None, :], tile_counts[None, :], 0), axis=1)
        extra = counts - HEAD
        before = jnp.sum(jnp.where(order[None, :] < order[:, None], extra[None, :], 0), axis=1)
        slot = lax.iota(jnp.int32, tail)
        rank = jnp.where(slot[None, :] < extra[:, None], before[:, None] + slot[None, :], -1).reshape(-1)
        here = rank - step * CAP
        here = jnp.where((rank >= 0) & (here >= 0) & (here < CAP), here, -1)
        results = pipeline(CAP, place, here, x0, g0, received0, *halves, w_gate, w_up, w_down, sums)
        return step + 1, results

    rows = tiles * HEAD
    shapes = ((rows, width), (own_rows - rows, width), w_gate.shape, w_up.shape, w_down.shape)
    start = (jnp.int32(0), tuple(blank(shapes)))
    _, sums = lax.while_loop(lambda state: state[0] * CAP < jnp.maximum(live, 1), one_pass, start)
    out0, out1, grad_gate, grad_up, grad_down = sums
    input_grad = jnp.concatenate([out0.reshape(tiles, HEAD, width), out1.reshape(tiles, tail, width)], axis=1)
    return (input_grad.reshape(own_rows, width), grad_gate.T, grad_up.T, grad_down)


def solution(mesh):
    fine = Mesh(mesh.devices.reshape(4, 2, 2, 4, 2), ("y", "xl", "xh", "z", "c"))
    row, col = ("y", "xl"), ("xh", "z", "c")
    in_specs = (P(col, row), P(col, row), P(), P(row, col), P(row, col), P(col, row))
    out_specs = (P(col, row), P(row, col), P(row, col), P(col, row))
    return jax.shard_map(shards, mesh=fine, in_specs=in_specs, out_specs=out_specs, check_vma=False)
```
